32 devices in a mesh: dp: 2 (over core), expert: 16 (over z, y, x).
Axes of the slice: x: 2, y: 2, z: 4, core: 2. Of those that a mesh axis runs over, the one named last changes fastest.
Arguments:
- tokens: bfloat16 [2, 32, 128, 2048], P(None, ('dp', 'expert')), may hold values from -6 to 6
- routes: int32 [2, 32, 128, 8], P(None, ('dp', 'expert')), may hold values from 0 to 15, all different within a row; in each aligned block of 128 rows (0 to 127, 128 to 255, ..., all dimensions but the last counted through in order) at most 72 rows name the same one
- prefix: int32 [2, 32], P(None, ('dp', 'expert')), may hold values from 12 to 64
- w_qkv: bfloat16 [2048, 6144], P(('dp', 'expert')), may hold values from -0.125 to 0.125
- w_out: bfloat16 [2048, 2048], P(('dp', 'expert')), may hold values from -0.75 to 0.75
- w_router: bfloat16 [2048, 16], P(('dp', 'expert')), may hold values from -0.02734375 to 0.02734375
- attn_gain: bfloat16 [2048], P(('dp', 'expert')), may hold values from 0.25 to 1.75
- ffn_gain: bfloat16 [2048], P(('dp', 'expert')), may hold values from 0.25 to 1.75
- query_gain: bfloat16 [2048], P(('dp', 'expert')), may hold values from 0.25 to 1.75
- key_gain: bfloat16 [2048], P(('dp', 'expert')), may hold values from 0.25 to 1.75
- w_gate: bfloat16 [16, 2048, 1024], P('expert'), may hold values from -0.125 to 0.125
- w_up: bfloat16 [16, 2048, 1024], P('expert'), may hold values from -0.125 to 0.125
- w_down: bfloat16 [16, 2048, 1024], P('expert'), may hold values from -1.5 to 1.5
- cotangent: bfloat16 [2, 32, 128, 2048], P(None, ('dp', 'expert')), may hold values from -6 to 6
Outputs:
- output: float32 [2, 32, 128, 2048], P(None, ('dp', 'expert'))
- input_grad: float32 [2, 32, 128, 2048], P(None, ('dp', 'expert'))
- grad_qkv: float32 [2048, 6144], P(('dp', 'expert'))
- grad_out: float32 [2048, 2048], P(('dp', 'expert'))
- grad_router: float32 [2048, 16], P(('dp', 'expert'))
- grad_attn_gain: float32 [2048], P(('dp', 'expert'))
- grad_ffn_gain: float32 [2048], P(('dp', 'expert'))
- grad_query_gain: float32 [2048], P(('dp', 'expert'))
- grad_key_gain: float32 [2048], P(('dp', 'expert'))
- grad_gate: float32 [16, 2048, 1024], P('expert', None, 'dp')
- grad_up: float32 [16, 2048, 1024], P('expert', None, 'dp')
- grad_down: float32 [16, 2048, 1024], P('expert', None, 'dp')
The draws below stay inside these ranges and needn't reach their ends.
Inputs may be any that keep to these rules, and one draw needn't show every extreme that they name: `routes`: each row names 8 different experts; among the 128 rows of one device in one micro-batch (aligned blocks of 128 positions) no expert is named more than 72 times, a bound that some block reaches.
All inputs are finite; a program needn't handle non-finite values.
Results may differ from the reference program's by a relative error of at most 0.015.
Values may be sent and summed in bfloat16 or wider, within the bound.
No kernel may reach another device: no remote copies, remote signals or barrier semaphores. Data moves between devices by JAX's collectives and lax.ppermute only.
A program may use at most 320 MiB of HBM per device.

```python
import math
import jax
import jax.numpy as jnp
import numpy as np
from jax import lax

D = 2048
H = 16
HD = 128
FF = 1024
TOP = 8
MB = 2
ROWS = 128
EXPERTS = 16
SEQ = 128
SEQS = 32
CAP = 72


def draw_prefix(key, part):
    values = jax.random.randint(key, (MB, SEQS), SEQ // 10, SEQ // 2 + 1, dtype=jnp.int32)
    values = values.at[0, 0].set(SEQ // 2)
    return values.at[MB - 1, SEQS - 1].set(SEQ // 10)


def with_spikes(result, stream_key, source, target, parts, factor):
    owner, partner = [(jnp.arange(result.shape[axis_at]) // (result.shape[axis_at] // parts)).reshape([-1 if axis == axis_at else 1 for axis in range(result.ndim)]) for axis_at in (source, target)]
    chosen = jax.random.permutation(stream_key, parts)[partner]
    strong = (owner == chosen) | (owner == (partner + parts // 2) % parts)
    return jnp.where(strong, factor * result, result)


def steps_of(rng, shape, pieces, low, top_value):
    def one(position, parts):
        draws = jax.random.uniform(jax.random.fold_in(jax.random.fold_in(rng, 6), position), (parts,), jnp.float32, low / len(pieces), top_value / len(pieces))
        return jnp.repeat(jnp.exp(draws), shape[position] // parts).reshape((-1,) + (1,) * (len(shape) - position - 1))

    level = one(*pieces[0])
    for cut in pieces[1:]:
        level = level * one(*cut)
    return level


def routed_block(rng, own, number, rows, count, top, most, lean):
    ranking = jax.random.permutation(rng, count)
    heavy_load, usual = load_shares(count, rows * top, most, lean, True), load_shares(count, rows * top, most, lean, False)
    places = jnp.arange(count)

    def named(lengths, turn):
        used = int((lengths > 0).sum())
        fixed = max(1, used // 4)
        moved = fixed + (places - fixed + turn * (used - fixed)) % max(1, count - fixed)
        return jnp.zeros((count,), jnp.int32).at[ranking[jnp.where(places < fixed, places, moved)]].set(jnp.asarray(lengths, jnp.int32))

    lengths = jnp.where(number % 4 == 0, named(heavy_load, number // 4), named(usual, number - number // 4 - 1))
    mixed = jax.random.permutation(jax.random.fold_in(own, 3), count)
    source_of, sink = mixed[0:count // 2 * 2:2], mixed[1:count // 2 * 2:2]
    slack = jnp.minimum(lengths[source_of] - 1, most - lengths[sink]) // 2
    slack = jnp.where((source_of == ranking[0]) | (sink == ranking[0]) | (lengths[sink] == 0), 0, jnp.maximum(slack, 0))
    moved = jax.random.randint(jax.random.fold_in(own, 4), (count // 2,), 0, 1 << 20) % (slack + 1)
    lengths = lengths.at[source_of].add(-moved).at[sink].add(moved)
    items = jnp.searchsorted(jnp.cumsum(lengths), jnp.arange(rows * top), side="right").astype(jnp.int32)
    grid = items.reshape(top, rows).T
    grid = grid[jax.random.permutation(jax.random.fold_in(own, 1), rows)]
    turn = jax.random.randint(jax.random.fold_in(own, 2), (rows, 1), 0, top)
    return jnp.take_along_axis(grid, (jnp.arange(top)[None, :] + turn) % top, axis=1)


def load_shares(number_of, total, bound, lean, full):
    loads = [(1 << 20) // math.isqrt(rank ** lean) + 1 for rank in range(1, number_of + 1)]
    largest = bound if full else min(bound, max(-(-total // number_of), total * loads[0] // sum(loads)))
    least = 1 if total - largest >= number_of - 1 else 0
    holding, rest = [largest] + [least] * (number_of - 1), total - largest - least * (number_of - 1)
    while rest > 0:
        free = [i for i in range(1, number_of) if holding[i] < largest] or [i for i in range(1, number_of) if holding[i] < bound]
        mass, budget = sum([loads[i] for i in free]), rest
        for i in free:
            more = min(bound - holding[i], max(1, budget * loads[i] // mass), rest)
            holding[i] = holding[i] + more
            rest = rest - more
    return np.array(holding)


def centred(stream_key, shape, deviation, limit, pieces=(), kind=jnp.bfloat16):
    entries = deviation * jax.random.normal(stream_key, shape, jnp.float32)
    if pieces:
        entries = entries * steps_of(stream_key, shape, pieces, -0.22, 0.18)
    return jnp.clip(entries, -limit, limit).astype(kind)


def gaussian_with(own_key, shape, scale, most, split, heavy, kind=jnp.bfloat16):
    array = scale * jax.random.normal(own_key, shape, jnp.float32)
    if split:
        array = array * steps_of(own_key, shape, split, -0.22, 0.18)
    return jnp.clip(with_spikes(array, jax.random.fold_in(own_key, 3), *heavy), -most, most).astype(kind)


def setup_inputs(seed: int = 0) -> dict:
    arg_keys = jax.random.split(jax.random.key(seed), 15)
    tokens = gaussian_with(arg_keys[0], (MB, SEQS, SEQ, D), 1.0, 6.0, ((1, 32),), (1, 3, 32, 2.75))
    routes_keys = jax.random.split(jax.random.fold_in(arg_keys[1], 1), MB * SEQS * SEQ // ROWS)
    routes_turns = jax.random.permutation(jax.random.fold_in(arg_keys[1], 3), MB * SEQS * SEQ // ROWS)
    routes = jax.vmap(lambda own, number: routed_block(jax.random.fold_in(arg_keys[1], 2), own, number, ROWS, EXPERTS, TOP, CAP, 2))(routes_keys, routes_turns).reshape((MB, SEQS, SEQ, TOP))
    prefix = draw_prefix(jax.random.fold_in(arg_keys[14], 71), 0)
    w_qkv = centred(arg_keys[3], (D, 3 * D), D ** -0.5, 0.125, ((0, 32),))
    w_out = centred(arg_keys[4], (D, D), (D // 32) ** -0.5, 0.75, ((0, 32),))
    w_router = centred(arg_keys[5], (D, EXPERTS), (25 * D) ** -0.5, 0.02734375, ((0, 32),))
    attn_gain = jnp.clip(1.0 + 0.15 * jax.random.normal(arg_keys[6], (D,), jnp.float32), 0.25, 1.75).astype(jnp.bfloat16)
    ffn_gain = jnp.clip(1.0 + 0.15 * jax.random.normal(arg_keys[7], (D,), jnp.float32), 0.25, 1.75).astype(jnp.bfloat16)
    query_gain = jnp.clip(1.0 + 0.15 * jax.random.normal(arg_keys[8], (D,), jnp.float32), 0.25, 1.75).astype(jnp.bfloat16)
    key_gain = jnp.clip(1.0 + 0.15 * jax.random.normal(arg_keys[9], (D,), jnp.float32), 0.25, 1.75).astype(jnp.bfloat16)
    w_gate = centred(arg_keys[10], (EXPERTS, D, FF), D ** -0.5, 0.125, ((0, 16),))
    w_up = centred(arg_keys[11], (EXPERTS, D, FF), D ** -0.5, 0.125, ((0, 16),))
    w_down = centred(arg_keys[12], (EXPERTS, D, FF), (max(1, FF // 64)) ** -0.5, 1.5, ((0, 16),))
    cotangent = centred(arg_keys[13], (MB, SEQS, SEQ, D), 1.0, 6.0, ((1, 32),))
    return dict(tokens=tokens, routes=routes, prefix=prefix, w_qkv=w_qkv, w_out=w_out, w_router=w_router, attn_gain=attn_gain, ffn_gain=ffn_gain, query_gain=query_gain, key_gain=key_gain, w_gate=w_gate, w_up=w_up, w_down=w_down, cotangent=cotangent)


@jax.custom_vjp
def low(v):
    return lax.optimization_barrier(v.astype(jnp.bfloat16)).astype(jnp.float32)

@jax.custom_vjp
def low_back(v):
    return v

def low_keep(v):
    return (low(v), None)

def low_pass(kept, grad):
    return (grad,)

def back_keep(v):
    return (v, None)

def back_low(kept, grad):
    return (low(grad),)
low.defvjp(low_keep, low_pass)
low_back.defvjp(back_keep, back_low)
epsilon = 1e-05
theta_base = 10000.0
masked_value = -1e+30
highest = lax.Precision.HIGHEST

def rms_scale(values):
    return lax.rsqrt(lax.optimization_barrier(jnp.mean(values * values, axis=-1, keepdims=True)) + epsilon)

def rope_tables(count, offset, width):
    halfway = width // 2
    inverse = theta_base ** (-(jnp.arange(halfway, dtype=jnp.float32) * 2.0) / width)
    places = offset + jnp.arange(count, dtype=jnp.float32)
    angles = places[:, None] * inverse[None, :]
    angles = jnp.concatenate([angles, angles], axis=1)
    return (jnp.cos(angles), jnp.sin(angles))

def rotate(values, cosine, sine):
    halfway = values.shape[-1] // 2
    turned = jnp.concatenate([-values[..., halfway:], values[..., :halfway]], axis=-1)
    return values * cosine[:, None, :] + turned * sine[:, None, :]

def attend(item):
    queries, keys_in, values_in, limits = item
    products = jnp.einsum('gqhd,gkhd->ghqk', queries, keys_in, precision=highest)
    scores = low_back(products) * HD ** (-0.5)
    places = jnp.arange(SEQ, dtype=jnp.int32)
    allowed = (places[None, None, :] <= places[None, :, None]) | (places[None, None, :] < limits[:, None, None])
    scores = jnp.where(allowed[:, None, :, :], scores, masked_value)
    weights = jax.nn.softmax(scores, axis=-1)
    return jnp.einsum('ghqk,gkhd->gqhd', low(weights), values_in, precision=highest)

def expert_rows(item):
    inputs, gate_w, up_w, down_w = item
    gate_val = low_back(jnp.dot(inputs, gate_w, precision=highest))
    up_val = low_back(jnp.dot(inputs, up_w, precision=highest))
    hidden = low(jax.nn.silu(gate_val) * up_val)
    return low(low_back(jnp.dot(hidden, down_w.T, precision=highest)))

def slot_tables(route_block):
    flat_routes = route_block.reshape(ROWS * TOP).astype(jnp.int32)
    onehot = (flat_routes[:, None] == jnp.arange(EXPERTS, dtype=jnp.int32)[None, :]).astype(jnp.int32)
    rank_of = (jnp.cumsum(onehot, axis=0) - 1).astype(jnp.int32)
    places = lax.optimization_barrier(jnp.sum(onehot * rank_of, axis=1)).astype(jnp.int32)
    slot_ids = (flat_routes * CAP + places).astype(jnp.int32)
    owners = jnp.full((EXPERTS * CAP,), ROWS * TOP, jnp.int32).at[slot_ids].set(jnp.arange(ROWS * TOP, dtype=jnp.int32))
    return (slot_ids, owners)

def take_rows(table, picks):
    return table[picks]

def reference(tokens, routes, prefix, w_qkv, w_out, w_router, attn_gain, ffn_gain, query_gain, key_gain, w_gate, w_up, w_down, cotangent):
    count = MB * SEQS * SEQ
    blocks = count // ROWS
    sequences = MB * SEQS
    group = math.gcd(sequences, max(1, 4096 // SEQ))
    route_blocks = routes.reshape(blocks, ROWS, TOP).astype(jnp.int32)
    slot_ids, owners = jax.vmap(slot_tables)(route_blocks)
    token_ids = (owners // TOP).astype(jnp.int32)
    flat_routes = routes.reshape(count, TOP).astype(jnp.int32)
    limits = prefix.reshape(sequences // group, group).astype(jnp.int32)
    cosine, sine = rope_tables(SEQ, 0.0, HD)

    def layer(resid, wqkv, wout, wrouter, gain_one, gain_two, gain_query, gain_key, wgate, wup, wdown):
        normed = low(resid * rms_scale(resid) * gain_one)
        mixed_in = low_back(jnp.dot(normed, wqkv, precision=highest))
        query = mixed_in[:, :D]
        keyed = mixed_in[:, D:2 * D]
        valued = mixed_in[:, 2 * D:]
        query = query * rms_scale(query) * gain_query
        keyed = keyed * rms_scale(keyed) * gain_key
        split_shape = (sequences // group, group, SEQ, H, HD)
        q_heads = low(rotate(query.reshape(sequences, SEQ, H, HD), cosine, sine)).reshape(split_shape)
        k_heads = low(rotate(keyed.reshape(sequences, SEQ, H, HD), cosine, sine)).reshape(split_shape)
        v_heads = low(valued).reshape(split_shape)
        attended = lax.map(jax.checkpoint(attend), (q_heads, k_heads, v_heads, limits))
        attended = low(low_back(attended.reshape(count, D)))
        hidden_one = resid + low_back(jnp.dot(attended, wout, precision=highest))
        normed_two = low(hidden_one * rms_scale(hidden_one) * gain_two)
        logits = low_back(jnp.dot(normed_two, wrouter, precision=highest))
        router = jax.nn.softmax(logits, axis=-1)
        weight = jnp.take_along_axis(router, flat_routes, axis=1)
        padded = jnp.concatenate([normed_two.reshape(blocks, ROWS, D), jnp.zeros((blocks, 1, D), jnp.float32)], axis=1)
        sent = low_back(jax.vmap(take_rows)(padded, token_ids))
        by_expert = sent.reshape(blocks, EXPERTS, CAP, D).transpose(1, 0, 2, 3).reshape(EXPERTS, blocks * CAP, D)
        results = lax.map(jax.checkpoint(expert_rows), (by_expert, wgate, wup, wdown))
        results = results.reshape(EXPERTS, blocks, CAP, D).transpose(1, 0, 2, 3).reshape(blocks, EXPERTS * CAP, D)
        picked = jax.vmap(take_rows)(results, slot_ids).reshape(count, TOP, D)
        return hidden_one + lax.optimization_barrier(jnp.sum(weight[:, :, None] * picked, axis=1))
    output, pullback = jax.vjp(layer, tokens.reshape(count, D).astype(jnp.float32), w_qkv.astype(jnp.float32), w_out.astype(jnp.float32), w_router.astype(jnp.float32), attn_gain.astype(jnp.float32), ffn_gain.astype(jnp.float32), query_gain.astype(jnp.float32), key_gain.astype(jnp.float32), w_gate.astype(jnp.float32), w_up.astype(jnp.float32), w_down.astype(jnp.float32))
    gradients = pullback(cotangent.reshape(count, D).astype(jnp.float32))
    return (output.reshape(MB, SEQS, SEQ, D), gradients[0].reshape(MB, SEQS, SEQ, D), gradients[1], gradients[2], gradients[3], gradients[4], gradients[5], gradients[6], gradients[7], gradients[8], gradients[9], gradients[10])
```

```python
import jax
import jax.numpy as jnp
import numpy as np
from jax import lax
from jax.sharding import PartitionSpec as P

HD = 128
TOP = 8


epsilon = 1e-05
theta_base = 10000.0
masked_value = -1e30
bf16 = jnp.bfloat16
f32 = jnp.float32


def rms_scale(values):
    return lax.rsqrt(jnp.mean(values * values, axis=-1, keepdims=True) + epsilon)


def rope_tables(count, offset, width):
    halfway = width // 2
    inverse = theta_base ** (-(jnp.arange(halfway, dtype=f32) * 2.0) / width)
    places = offset + jnp.arange(count, dtype=f32)
    angles = places[:, None] * inverse[None, :]
    angles = jnp.concatenate([angles, angles], axis=1)
    return (jnp.cos(angles), jnp.sin(angles))


def rotate(values, cosine, sine):
    halfway = values.shape[-1] // 2
    turned = jnp.concatenate([-values[..., halfway:], values[..., :halfway]], axis=-1)
    return values * cosine[:, None, :] + turned * sine[:, None, :]


def norm_back(incoming, values, scaling, gain):
    weighted = incoming * gain
    inner = jnp.mean(weighted * values, axis=-1, keepdims=True)
    d_values = scaling * weighted - values * scaling * scaling * scaling * inner
    return (d_values, jnp.sum(incoming * values * scaling, axis=0))


def add_low(one, two):
    return (one.astype(f32) + two.astype(f32)).astype(one.dtype)


class Grid:
    def __init__(self, owners):
        self.owners = owners
        self.dims = {16: (4, 2, 2), 64: (4, 4, 4)}.get(owners, (owners, 1, 1))
        self.strides = (self.dims[1] * self.dims[2], self.dims[2], 1)

    def place(self):
        index = lax.axis_index("expert")
        return [index // s % n for s, n in zip(self.strides, self.dims)]

    def shift(self, values, axis, by):
        n, s = self.dims[axis], self.strides[axis]
        pairs = []
        for i in range(self.owners):
            c = i // s % n
            pairs.append((i, i + ((c + by) % n - c) * s))
        return lax.ppermute(values, "expert", pairs)

    def gather(self, values, axis):
        n = self.dims[axis]
        out = [values] + [None] * (n - 1)
        ahead = n // 2
        for k in range(1, ahead + 1):
            out[k] = self.shift(out[k - 1], axis, 1)
        for k in range(1, n - ahead):
            out[n - k] = self.shift(out[(n - k + 1) % n], axis, -1)
        return out

    def scatter(self, parts, axis, last=False):
        n = self.dims[axis]
        ahead = n // 2
        arrived = []
        if ahead:
            total = parts[ahead]
            for k in range(ahead - 1, -1, -1):
                total = self.shift(total, axis, -1)
                if k:
                    total = add_low(total, parts[k])
            arrived.append(total)
        if n - 1 - ahead:
            total = parts[ahead + 1]
            for k in range(ahead + 2, n + 1):
                total = self.shift(total, axis, 1)
                if k < n:
                    total = add_low(total, parts[k])
            arrived.append(total)
        total = parts[0].astype(f32)
        for other in arrived:
            total = total + other.astype(f32)
        return total if last else total.astype(parts[0].dtype)


def swap(values):
    return lax.ppermute(values, "dp", [(0, 1), (1, 0)])


def gather_weight(grid, shard):
    half = shard.shape[0] // 2
    columns = shard.shape[1]
    pieces = []
    for part, first, second in ((shard[:half], 2, 1), (shard[half:], 1, 2)):
        line = jnp.stack(grid.gather(part, 0))
        plane = jnp.stack(grid.gather(line, first))
        for piece in grid.gather(plane, second):
            pieces.append(piece.reshape(-1, columns))
    others = [swap(piece) for piece in pieces]
    return jnp.concatenate(pieces + others, axis=0)


def weight_order(grid, shard_rows):
    nz, ny, nx = grid.dims
    half = shard_rows // 2
    z, y, x = grid.place()
    core = lax.axis_index("dp")
    tables = []
    for dp_r in range(2):
        a = np.stack(np.meshgrid(np.arange(ny), np.arange(nx), np.arange(nz), np.arange(half), indexing="ij"), -1).reshape(-1, 4)
        b = np.stack(np.meshgrid(np.arange(nx), np.arange(ny), np.arange(nz), np.arange(half), indexing="ij"), -1).reshape(-1, 4)
        for color, (ry, rx, rz, i) in ((0, a.T), (1, (b.T[1], b.T[0], b.T[2], b.T[3]))):
            tables.append(np.stack([np.full_like(ry, dp_r), rz, ry, rx, i + color * half]))
    t = np.concatenate(tables, axis=1).astype(np.int32)
    where = ((core + 2 - t[0]) % 2) * grid.owners
    where = where + ((z + nz - t[1]) % nz) * grid.strides[0]
    where = where + ((y + ny - t[2]) % ny) * grid.strides[1] + (x + nx - t[3]) % nx
    return (where * shard_rows + t[4]).astype(jnp.int32)


def scatter_rows(grid, kept):
    nz, ny, nx = grid.dims
    rows, columns = kept.shape
    out = []
    for part, first, second in ((kept[: rows // 2], 1, 2), (kept[rows // 2 :], 2, 1)):
        part = part.reshape(grid.dims[first], -1, columns)
        part = grid.scatter([part[k] for k in range(grid.dims[first])], first)
        part = part.reshape(grid.dims[second], -1, columns)
        part = grid.scatter([part[k] for k in range(grid.dims[second])], second)
        part = part.reshape(nz, -1, columns)
        out.append(grid.scatter([part[k] for k in range(nz)], 0, last=True))
    return jnp.concatenate(out, axis=0)


def reduce_product(grid, left, right):
    half = left.shape[1] // 2
    product = lambda a: lax.dot_general(a, right, (((0,), (0,)), ((), ())), preferred_element_type=f32)
    far = swap(product(left[:, half:]).astype(bf16))
    near = (product(left[:, :half]) + far.astype(f32)).astype(bf16)
    return scatter_rows(grid, near)


def reduce_small(grid, values):
    half = values.shape[0] // 2
    return scatter_rows(grid, values[:half] + swap(values[half:]))


def dispatch(grid, values, slots_own, slots_y, slots_x):
    nz, ny, nx = grid.dims
    rows, width = values.shape
    h = width // 2
    pack = lambda table, blocks: lax.dot_general(
        table, blocks, (((3,), (2,)), ((0, 1), (0, 1))), preferred_element_type=f32
    ).astype(bf16)
    line = jnp.stack(grid.gather(values, 0))
    plane = jnp.stack(grid.gather(line[..., :h], 2))
    left = [pack(slots_own[0], plane)]
    for k in range(1, ny):
        left.append(grid.shift(pack(slots_y[k - 1], plane), 1, k))
    plane = jnp.stack(grid.gather(line[..., h:], 1))
    right = [pack(slots_own[:, 0], plane)]
    for k in range(1, nx):
        right.append(grid.shift(pack(slots_x[k - 1], plane), 2, k))
    return jnp.concatenate([jnp.stack(left), jnp.stack(right, axis=1)], axis=-1)


def combine(grid, packed, h, slots_own, slots_y, slots_x):
    nz, ny, nx = grid.dims
    unpack = lambda table, blocks: lax.dot_general(
        table, blocks, (((2,), (2,)), ((0, 1), (0, 1))), preferred_element_type=f32
    ).astype(bf16)
    left = [packed[0, ..., :h]]
    for k in range(1, ny):
        left.append(grid.shift(packed[k, ..., :h], 1, -k))
    table = jnp.concatenate([slots_own[0]] + [slots_y[k - 1] for k in range(1, ny)], axis=2)
    plane = unpack(table, jnp.concatenate(left, axis=2))
    left = grid.scatter([plane[k] for k in range(nx)], 2)
    right = [packed[:, 0, ..., h:]]
    for k in range(1, nx):
        right.append(grid.shift(packed[:, k, ..., h:], 2, -k))
    table = jnp.concatenate([slots_own[:, 0]] + [slots_x[k - 1] for k in range(1, nx)], axis=2)
    plane = unpack(table, jnp.concatenate(right, axis=2))
    right = grid.scatter([plane[k] for k in range(ny)], 1)
    line = jnp.concatenate([left, right], axis=-1)
    return grid.scatter([line[k] for k in range(nz)], 0, last=True)


def shards(
    grid,
    tokens,
    routes,
    prefix,
    w_qkv,
    w_out,
    w_router,
    attn_gain,
    ffn_gain,
    query_gain,
    key_gain,
    w_gate,
    w_up,
    w_down,
    cotangent,
):
    micro = tokens.shape[0]
    rows = tokens.shape[2]
    width = tokens.shape[3]
    shard_rows = w_qkv.shape[0]
    experts = w_router.shape[1]
    nz, ny, nx = grid.dims
    heads = width // HD
    count = micro * rows
    capacity = max(2, rows * TOP * 9 // (experts * 8))
    scaling = HD ** (-0.5)
    cosine, sine = rope_tables(rows, 0.0, HD)
    positions = jnp.arange(rows, dtype=jnp.int32)
    numbers = jnp.arange(experts, dtype=jnp.int32)
    core = lax.axis_index("dp")
    me = lax.axis_index("expert")
    z, y, x = grid.place()

    lanes = rows
    small = jnp.concatenate(
        [w_router] + [gain[:, None] for gain in (attn_gain, ffn_gain, query_gain, key_gain)], axis=1
    )
    small = jnp.pad(small, ((0, 0), (0, lanes - small.shape[1])))
    member = jnp.any(routes[:, 0, None, :, :] == numbers[None, :, None, None], axis=-1)
    member = member.astype(bf16).reshape(micro * experts, rows)
    table = jnp.concatenate([small, member], axis=0)
    table = jnp.stack(grid.gather(table, 0))
    table = jnp.stack(grid.gather(table, 2))
    table = jnp.stack(grid.gather(table, 1))
    small = table[:, :, :, :shard_rows].reshape(-1, lanes)
    small = jnp.concatenate([small, swap(small)], axis=0)
    t = np.stack(
        np.meshgrid(*[np.arange(n) for n in (2, ny, nx, nz, shard_rows)], indexing="ij"), -1
    ).reshape(-1, 5).T.astype(np.int32)
    where = ((core + 2 - t[0]) % 2) * grid.owners + ((z + nz - t[3]) % nz) * grid.strides[0]
    where = where + ((y + ny - t[1]) % ny) * grid.strides[1] + (x + nx - t[2]) % nx
    where = where * shard_rows + t[4]
    features = jnp.arange(width, dtype=jnp.int32)
    spot = (features[:, None] == where[None, :]).astype(bf16)
    small = jnp.dot(spot, small, preferred_element_type=f32)
    wrouter = small[:, :experts].astype(bf16)
    gain_one, gain_two, gain_query, gain_key = [small[:, experts + k] for k in range(4)]
    member = table[:, :, :, shard_rows:].reshape(ny, nx, nz, micro, experts, rows)
    triangle = (positions[:, None] <= positions[None, :]).astype(bf16)
    ranks = jnp.dot(member, triangle, preferred_element_type=f32).astype(jnp.int32) - 1
    ranks = jnp.where(member > 0, ranks, -1)
    ranks = jnp.transpose(ranks, (4, 3, 0, 1, 2, 5))
    slot_numbers = jnp.arange(capacity, dtype=jnp.int32)
    expand = lambda r: (r[..., None, :] == slot_numbers[:, None]).astype(bf16)
    pick = lambda e: lax.dynamic_index_in_dim(ranks, e, 0, keepdims=False)
    near = lambda dy, dx: (z * ny + (y + dy) % ny) * nx + (x + dx) % nx
    slots_own = expand(pick(me))
    slots_y = [expand(pick(near(k, 0))[:, 0]) for k in range(1, ny)]
    slots_x = [expand(pick(near(0, k))[:, :, 0]) for k in range(1, nx)]
    tables = [
        (slots_own[m], [s[m] for s in slots_y], [s[m] for s in slots_x]) for m in range(micro)
    ]

    order = weight_order(grid, shard_rows)
    turn = (features[:, None] == order[None, :]).astype(bf16)
    to_order = lambda v: jnp.dot(v, turn, preferred_element_type=f32).astype(bf16)
    from_order = lambda v: lax.dot_general(
        v, turn, (((1,), (1,)), ((), ())), preferred_element_type=f32
    )

    w_parts = [gather_weight(grid, w_qkv[:, k * width : (k + 1) * width]) for k in range(3)]
    wout = gather_weight(grid, w_out)
    incoming_rows = [dispatch(grid, cotangent[m, 0], *tables[m]) for m in range(micro)]

    resid = tokens.astype(f32).reshape(count, width)
    scale_one = rms_scale(resid)
    normed = to_order((resid * scale_one * gain_one).astype(bf16))
    query, keyed, valued = [jnp.dot(normed, w, preferred_element_type=f32) for w in w_parts]
    scale_query = rms_scale(query)
    scale_key = rms_scale(keyed)
    split = lambda v: v.reshape(micro, rows, heads, HD)
    q_heads = rotate(split(query * scale_query * gain_query), cosine, sine).astype(bf16)
    k_all = rotate(split(keyed * scale_key * gain_key), cosine, sine).astype(bf16)
    v_all = split(valued).astype(bf16)
    allowed = (positions[None, None, :] <= positions[None, :, None]) | (
        positions[None, None, :] < prefix[:, 0][:, None, None]
    )
    scores = jnp.einsum("bqhd,bkhd->bhqk", q_heads, k_all, preferred_element_type=f32) * scaling
    scores = jnp.where(allowed[:, None], scores, masked_value)
    expo = jnp.exp(scores - jnp.max(scores, axis=-1, keepdims=True))
    probs = expo / jnp.sum(expo, axis=-1, keepdims=True)
    attended = jnp.einsum("bhqk,bkhd->bqhd", probs.astype(bf16), v_all, preferred_element_type=f32)
    attended = to_order(attended.reshape(count, width).astype(bf16))
    hidden_one = resid + jnp.dot(attended, wout, preferred_element_type=f32)
    scale_two = rms_scale(hidden_one)
    normed_two = (hidden_one * scale_two * gain_two).astype(bf16)
    router = jax.nn.softmax(jnp.dot(normed_two, wrouter, preferred_element_type=f32), axis=-1)

    blocks = ny * nx * nz * capacity
    h = width // 2
    grads = []
    d_rows_back = []
    outputs_back = []
    for m in range(micro):
        row_in = dispatch(grid, normed_two[m * rows : (m + 1) * rows], *tables[m])
        row_in = row_in.reshape(blocks, width)
        g_in = incoming_rows[m].reshape(blocks, width)
        share = jax.nn.softmax(jnp.dot(row_in, wrouter, preferred_element_type=f32), axis=-1)
        share = jnp.sum(jnp.where(numbers[None, :] == me, share, 0.0), axis=-1, keepdims=True)
        gate_val = jnp.dot(row_in, w_gate[0], preferred_element_type=f32)
        up_val = jnp.dot(row_in, w_up[0], preferred_element_type=f32)
        back = jnp.dot(g_in, w_down[0], preferred_element_type=f32)
        sigmoid_val = jax.nn.sigmoid(gate_val)
        activated = gate_val * sigmoid_val
        hidden = (activated * up_val).astype(bf16)
        d_share = jnp.sum(hidden.astype(f32) * back, axis=-1, keepdims=True)
        d_hidden = back * share
        d_gate = (d_hidden * up_val * sigmoid_val * (1.0 + gate_val * (1.0 - sigmoid_val))).astype(bf16)
        d_up = (d_hidden * activated).astype(bf16)
        hidden_share = (hidden.astype(f32) * share).astype(bf16)
        times_t = lambda a, b: lax.dot_general(a, b, (((1,), (1,)), ((), ())), preferred_element_type=f32)
        d_rows = (times_t(d_gate, w_gate[0]) + times_t(d_up, w_up[0])).astype(bf16)
        high = d_share.astype(bf16)
        low = (d_share - high.astype(f32)).astype(bf16)
        at = jnp.arange(2 * experts if 2 * experts > 128 else 128, dtype=jnp.int32)[None, :]
        extra = jnp.where(at == me, high, jnp.where(at == me + experts, low, 0.0)).astype(bf16)
        d_rows = jnp.concatenate([extra, d_rows], axis=1).reshape(ny, nx, nz, capacity, -1)
        d_rows_back.append(combine(grid, d_rows, h + extra.shape[1], *tables[m]))
        out_rows = (times_t(hidden, w_down[0]) * share).astype(bf16)
        out_rows = out_rows.reshape(ny, nx, nz, capacity, width)
        outputs_back.append(combine(grid, out_rows, h, *tables[m]))
        across = lambda a, b: lax.dot_general(a, b, (((0,), (0,)), ((), ())), preferred_element_type=f32)
        grads.append((across(row_in, d_gate), across(row_in, d_up), across(g_in, hidden_share)))
    extra_width = d_rows_back[0].shape[1] - width
    output = hidden_one + jnp.concatenate(outputs_back, axis=0)
    half = w_gate.shape[2] // 2
    expert_grads = []
    for one, two in zip(*grads):
        total = one + two
        far = lax.dynamic_slice_in_dim(total, (1 - core) * half, half, axis=1)
        near_half = lax.dynamic_slice_in_dim(total, core * half, half, axis=1)
        expert_grads.append((near_half + swap(far.astype(bf16)).astype(f32))[None])

    incoming = cotangent.astype(f32).reshape(count, width)
    returned = jnp.concatenate(d_rows_back, axis=0)
    d_router = returned[:, :experts] + returned[:, experts : 2 * experts]
    d_logits = (router * (d_router - jnp.sum(router * d_router, axis=-1, keepdims=True))).astype(bf16)
    d_normed_two = returned[:, extra_width:] + jnp.einsum(
        "re,de->rd", d_logits, wrouter, preferred_element_type=f32
    )
    grad_route = jnp.einsum("rd,re->de", normed_two, d_logits, preferred_element_type=f32)
    d_norm_two, sum_two = norm_back(d_normed_two, hidden_one, scale_two, gain_two)
    d_hidden_one = incoming + d_norm_two
    d_branch = d_hidden_one.astype(bf16)
    grad_wout = reduce_product(grid, attended, d_branch)

    d_mixed = lax.dot_general(d_branch, wout, (((1,), (1,)), ((), ())), preferred_element_type=f32)
    d_mixed = split(from_order(d_mixed.astype(bf16)).astype(bf16))
    d_probs = jnp.einsum("bqhd,bkhd->bhqk", d_mixed, v_all, preferred_element_type=f32)
    d_values = jnp.einsum("bhqk,bqhd->bkhd", probs.astype(bf16), d_mixed, preferred_element_type=f32)
    d_scores = (
        probs * (d_probs - jnp.sum(probs * d_probs, axis=-1, keepdims=True)) * scaling
    ).astype(bf16)
    d_queries = jnp.einsum("bhqk,bkhd->bqhd", d_scores, k_all, preferred_element_type=f32)
    d_keys = jnp.einsum("bhqk,bqhd->bkhd", d_scores, q_heads, preferred_element_type=f32)
    d_query_normed = rotate(d_queries, cosine, -sine).reshape(count, width)
    d_key_normed = rotate(d_keys, cosine, -sine).reshape(count, width)
    d_query, sum_query = norm_back(d_query_normed, query, scale_query, gain_query)
    d_key, sum_key = norm_back(d_key_normed, keyed, scale_key, gain_key)
    d_parts = [d_query.astype(bf16), d_key.astype(bf16), d_values.reshape(count, width).astype(bf16)]
    grad_parts = [reduce_product(grid, normed, part) for part in d_parts]
    d_normed = sum(
        lax.dot_general(part, w, (((1,), (1,)), ((), ())), preferred_element_type=f32)
        for part, w in zip(d_parts, w_parts)
    )
    d_high = d_normed.astype(bf16)
    d_low = (d_normed - d_high.astype(f32)).astype(bf16)
    d_normed = from_order(d_high) + from_order(d_low)
    d_resid, sum_one = norm_back(d_normed, resid, scale_one, gain_one)
    input_grad = d_hidden_one + d_resid

    sums = jnp.concatenate([grad_route, jnp.stack([sum_one, sum_two, sum_query, sum_key], axis=1)], axis=1)
    sums = jnp.pad(sums, ((0, 0), (0, lanes - sums.shape[1])))
    parts = []
    for _ in range(3):
        parts.append(sums.astype(bf16))
        sums = sums - parts[-1].astype(f32)
    sums = sum(
        lax.dot_general(turn, part, (((0,), (0,)), ((), ())), preferred_element_type=f32)
        for part in parts
    )
    sums = reduce_small(grid, sums)
    grad_gains = [sums[:, experts + k] for k in range(4)]

    shape = (micro, 1, rows, width)
    return (
        output.reshape(shape),
        input_grad.reshape(shape),
        jnp.concatenate(grad_parts, axis=1),
        grad_wout,
        sums[:, :experts],
        *grad_gains,
        *expert_grads,
    )


def solution(mesh):
    grid = Grid(mesh.shape["expert"])
    both = ("dp", "expert")
    tokens_spec = P(None, both, None, None)
    return jax.shard_map(
        lambda *args: shards(grid, *args),
        mesh=mesh,
        in_specs=(
            tokens_spec,
            tokens_spec,
            P(None, both),
            P(both, None),
            P(both, None),
            P(both, None),
            P(both),
            P(both),
            P(both),
            P(both),
            P("expert", None, None),
            P("expert", None, None),
            P("expert", None, None),
            tokens_spec,
        ),
        out_specs=(
            tokens_spec,
            tokens_spec,
            P(both, None),
            P(both, None),
            P(both, None),
            P(both),
            P(both),
            P(both),
            P(both),
            P("expert", None, "dp"),
            P("expert", None, "dp"),
            P("expert", None, "dp"),
        ),
        check_vma=False,
    )
```

```python
import jax
import jax.numpy as jnp
import numpy as np
from jax import lax
from jax.sharding import PartitionSpec as P

HD = 128
TOP = 8


epsilon = 1e-05
theta_base = 10000.0
masked_value = -1e30
bf16 = jnp.bfloat16
f32 = jnp.float32


def rms_scale(values):
    return lax.rsqrt(jnp.mean(values * values, axis=-1, keepdims=True) + epsilon)


def rope_tables(count, offset, width):
    halfway = width // 2
    inverse = theta_base ** (-(jnp.arange(halfway, dtype=f32) * 2.0) / width)
    places = offset + jnp.arange(count, dtype=f32)
    angles = places[:, None] * inverse[None, :]
    angles = jnp.concatenate([angles, angles], axis=1)
    return (jnp.cos(angles), jnp.sin(angles))


def rotate(values, cosine, sine):
    halfway = values.shape[-1] // 2
    turned = jnp.concatenate([-values[..., halfway:], values[..., :halfway]], axis=-1)
    return values * cosine[:, None, :] + turned * sine[:, None, :]


def norm_back(incoming, values, scaling, gain):
    weighted = incoming * gain
    inner = jnp.mean(weighted * values, axis=-1, keepdims=True)
    d_values = scaling * weighted - values * scaling * scaling * scaling * inner
    return (d_values, jnp.sum(incoming * values * scaling, axis=0))


def add_low(one, two):
    return (one.astype(f32) + two.astype(f32)).astype(one.dtype)


class Grid:
    def __init__(self, owners):
        self.owners = owners
        self.dims = {16: (4, 2, 2), 64: (4, 4, 4)}.get(owners, (owners, 1, 1))
        self.strides = (self.dims[1] * self.dims[2], self.dims[2], 1)

    def place(self):
        index = lax.axis_index("expert")
        return [index // s % n for s, n in zip(self.strides, self.dims)]

    def shift(self, values, axis, by):
        n, s = self.dims[axis], self.strides[axis]
        pairs = []
        for i in range(self.owners):
            c = i // s % n
            pairs.append((i, i + ((c + by) % n - c) * s))
        return lax.ppermute(values, "expert", pairs)

    def gather(self, values, axis):
        n = self.dims[axis]
        out = [values] + [None] * (n - 1)
        ahead = n // 2
        for k in range(1, ahead + 1):
            out[k] = self.shift(out[k - 1], axis, 1)
        for k in range(1, n - ahead):
            out[n - k] = self.shift(out[(n - k + 1) % n], axis, -1)
        return out

    def scatter(self, parts, axis, last=False):
        n = self.dims[axis]
        ahead = n // 2
        arrived = []
        if ahead:
            total = parts[ahead]
            for k in range(ahead - 1, -1, -1):
                total = self.shift(total, axis, -1)
                if k:
                    total = add_low(total, parts[k])
            arrived.append(total)
        if n - 1 - ahead:
            total = parts[ahead + 1]
            for k in range(ahead + 2, n + 1):
                total = self.shift(total, axis, 1)
                if k < n:
                    total = add_low(total, parts[k])
            arrived.append(total)
        total = parts[0].astype(f32)
        for other in arrived:
            total = total + other.astype(f32)
        return total if last else total.astype(parts[0].dtype)


def after(values, *others):
    return lax.optimization_barrier((values, *others))[0]


def swap(values):
    return lax.ppermute(values, "dp", [(0, 1), (1, 0)])


def gather_weight(grid, shard, *earlier):
    half = shard.shape[0] // 2
    columns = shard.shape[1]
    pieces = []
    along = grid.gather(after(shard, *earlier), 0)
    for part, first, second in ((slice(0, half), 2, 1), (slice(half, None), 1, 2)):
        line = jnp.stack([piece[part] for piece in along])
        plane = jnp.stack(grid.gather(line, first))
        for piece in grid.gather(plane, second):
            pieces.append(piece.reshape(-1, columns))
    own = jnp.concatenate(pieces, axis=0)
    return (own, swap(own)), along[1:]


def times(values, weight):
    half = weight[0].shape[0]
    return sum(
        jnp.dot(values[:, k * half : (k + 1) * half], weight[k], preferred_element_type=f32)
        for k in range(2)
    )


def times_turned(values, weight):
    return [
        lax.dot_general(values, part, (((1,), (1,)), ((), ())), preferred_element_type=f32)
        for part in weight
    ]


def weight_order(grid, shard_rows):
    nz, ny, nx = grid.dims
    half = shard_rows // 2
    z, y, x = grid.place()
    core = lax.axis_index("dp")
    tables = []
    for dp_r in range(2):
        a = np.stack(np.meshgrid(np.arange(ny), np.arange(nx), np.arange(nz), np.arange(half), indexing="ij"), -1).reshape(-1, 4)
        b = np.stack(np.meshgrid(np.arange(nx), np.arange(ny), np.arange(nz), np.arange(half), indexing="ij"), -1).reshape(-1, 4)
        for color, (ry, rx, rz, i) in ((0, a.T), (1, (b.T[1], b.T[0], b.T[2], b.T[3]))):
            tables.append(np.stack([np.full_like(ry, dp_r), rz, ry, rx, i + color * half]))
    t = np.concatenate(tables, axis=1).astype(np.int32)
    where = ((core + 2 - t[0]) % 2) * grid.owners
    where = where + ((z + nz - t[1]) % nz) * grid.strides[0]
    where = where + ((y + ny - t[2]) % ny) * grid.strides[1] + (x + nx - t[3]) % nx
    return (where * shard_rows + t[4]).astype(jnp.int32)


def scatter_rows(grid, kept):
    nz, ny, nx = grid.dims
    rows, columns = kept.shape
    out = []
    sums = []
    for part, first, second in ((kept[: rows // 2], 1, 2), (kept[rows // 2 :], 2, 1)):
        part = part.reshape(grid.dims[first], -1, columns)
        part = grid.scatter([part[k] for k in range(grid.dims[first])], first)
        part = part.reshape(grid.dims[second], -1, columns)
        sums.append(part)
        part = grid.scatter([part[k] for k in range(grid.dims[second])], second)
        part = part.reshape(nz, -1, columns)
        out.append(grid.scatter([part[k] for k in range(nz)], 0, last=True))
    return jnp.concatenate(out, axis=0), sums


def reduce_product(grid, left, right):
    half = left.shape[1] // 2
    product = lambda a: lax.dot_general(a, right, (((0,), (0,)), ((), ())), preferred_element_type=f32)
    sent = product(left[:, half:]).astype(bf16)
    near = (product(left[:, :half]) + swap(sent).astype(f32)).astype(bf16)
    shard, sums = scatter_rows(grid, near)
    return shard, sent, near, sums


def reduce_small(grid, values):
    half = values.shape[0] // 2
    return scatter_rows(grid, values[:half] + swap(values[half:]))[0]


def dispatch(grid, values, earlier, slots_own, slots_y, slots_x):
    nz, ny, nx = grid.dims
    rows, width = values.shape
    h = width // 2
    pack = lambda table, blocks: lax.dot_general(
        table, blocks, (((3,), (2,)), ((0, 1), (0, 1))), preferred_element_type=f32
    ).astype(bf16)
    along = grid.gather(after(values, *earlier), 0)
    line = jnp.stack(along)
    plane = jnp.stack(grid.gather(line[..., :h], 2))
    left = [pack(slots_own[0], plane)]
    for k in range(1, ny):
        left.append(grid.shift(pack(slots_y[k - 1], plane), 1, k))
    plane = jnp.stack(grid.gather(line[..., h:], 1))
    right = [pack(slots_own[:, 0], plane)]
    for k in range(1, nx):
        right.append(grid.shift(pack(slots_x[k - 1], plane), 2, k))
    return jnp.concatenate([jnp.stack(left), jnp.stack(right, axis=1)], axis=-1), along[1:]


def combine(grid, packed, h, earlier, slots_own, slots_y, slots_x):
    nz, ny, nx = grid.dims
    if earlier is not None:
        packed = after(packed, earlier)
    unpack = lambda table, blocks: lax.dot_general(
        table, blocks, (((2,), (2,)), ((0, 1), (0, 1))), preferred_element_type=f32
    ).astype(bf16)
    left = [packed[0, ..., :h]]
    for k in range(1, ny):
        left.append(grid.shift(packed[k, ..., :h], 1, -k))
    table = jnp.concatenate([slots_own[0]] + [slots_y[k - 1] for k in range(1, ny)], axis=2)
    plane = unpack(table, jnp.concatenate(left, axis=2))
    planes = [plane]
    left = grid.scatter([plane[k] for k in range(nx)], 2)
    right = [packed[:, 0, ..., h:]]
    for k in range(1, nx):
        right.append(grid.shift(packed[:, k, ..., h:], 2, -k))
    table = jnp.concatenate([slots_own[:, 0]] + [slots_x[k - 1] for k in range(1, nx)], axis=2)
    plane = unpack(table, jnp.concatenate(right, axis=2))
    planes.append(plane)
    right = grid.scatter([plane[k] for k in range(ny)], 1)
    line = jnp.concatenate([left, right], axis=-1)
    return grid.scatter([line[k] for k in range(nz)], 0, last=True), planes, line


def shards(
    grid,
    tokens,
    routes,
    prefix,
    w_qkv,
    w_out,
    w_router,
    attn_gain,
    ffn_gain,
    query_gain,
    key_gain,
    w_gate,
    w_up,
    w_down,
    cotangent,
):
    micro = tokens.shape[0]
    rows = tokens.shape[2]
    width = tokens.shape[3]
    shard_rows = w_qkv.shape[0]
    experts = w_router.shape[1]
    nz, ny, nx = grid.dims
    heads = width // HD
    count = micro * rows
    capacity = max(2, rows * TOP * 9 // (experts * 8))
    scaling = HD ** (-0.5)
    cosine, sine = rope_tables(rows, 0.0, HD)
    positions = jnp.arange(rows, dtype=jnp.int32)
    numbers = jnp.arange(experts, dtype=jnp.int32)
    core = lax.axis_index("dp")
    me = lax.axis_index("expert")
    z, y, x = grid.place()

    lanes = rows
    small = jnp.concatenate(
        [w_router] + [gain[:, None] for gain in (attn_gain, ffn_gain, query_gain, key_gain)], axis=1
    )
    small = jnp.pad(small, ((0, 0), (0, lanes - small.shape[1])))
    member = jnp.any(routes[:, 0, None, :, :] == numbers[None, :, None, None], axis=-1)
    member = member.astype(bf16).reshape(micro * experts, rows)
    table = jnp.concatenate([small, member], axis=0)
    table = jnp.stack(grid.gather(table, 0))
    table = jnp.stack(grid.gather(table, 2))
    table = jnp.stack(grid.gather(table, 1))
    small = table[:, :, :, :shard_rows].reshape(-1, lanes)
    small = jnp.concatenate([small, swap(small)], axis=0)
    t = np.stack(
        np.meshgrid(*[np.arange(n) for n in (2, ny, nx, nz, shard_rows)], indexing="ij"), -1
    ).reshape(-1, 5).T.astype(np.int32)
    where = ((core + 2 - t[0]) % 2) * grid.owners + ((z + nz - t[3]) % nz) * grid.strides[0]
    where = where + ((y + ny - t[1]) % ny) * grid.strides[1] + (x + nx - t[2]) % nx
    where = where * shard_rows + t[4]
    features = jnp.arange(width, dtype=jnp.int32)
    spot = (features[:, None] == where[None, :]).astype(bf16)
    small = jnp.dot(spot, small, preferred_element_type=f32)
    wrouter = small[:, :experts].astype(bf16)
    gain_one, gain_two, gain_query, gain_key = [small[:, experts + k] for k in range(4)]
    member = table[:, :, :, shard_rows:].reshape(ny, nx, nz, micro, experts, rows)
    triangle = (positions[:, None] <= positions[None, :]).astype(bf16)
    ranks = jnp.dot(member, triangle, preferred_element_type=f32).astype(jnp.int32) - 1
    ranks = jnp.where(member > 0, ranks, -1)
    ranks = jnp.transpose(ranks, (4, 3, 0, 1, 2, 5))
    slot_numbers = jnp.arange(capacity, dtype=jnp.int32)
    expand = lambda r: (r[..., None, :] == slot_numbers[:, None]).astype(bf16)
    pick = lambda e: lax.dynamic_index_in_dim(ranks, e, 0, keepdims=False)
    near = lambda dy, dx: (z * ny + (y + dy) % ny) * nx + (x + dx) % nx
    slots_own = expand(pick(me))
    slots_y = [expand(pick(near(k, 0))[:, 0]) for k in range(1, ny)]
    slots_x = [expand(pick(near(0, k))[:, :, 0]) for k in range(1, nx)]
    tables = [
        (slots_own[m], [s[m] for s in slots_y], [s[m] for s in slots_x]) for m in range(micro)
    ]

    order = weight_order(grid, shard_rows)
    turn = (features[:, None] == order[None, :]).astype(bf16)
    to_order = lambda v: jnp.dot(v, turn, preferred_element_type=f32).astype(bf16)
    from_order = lambda v: lax.dot_general(
        v, turn, (((1,), (1,)), ((), ())), preferred_element_type=f32
    )

    w_parts = []
    earlier = [table]
    for w in [w_qkv[:, k * width : (k + 1) * width] for k in range(3)] + [w_out]:
        gathered, earlier = gather_weight(grid, w, *earlier)
        w_parts.append(gathered)
    wout = w_parts.pop()
    incoming_rows = []
    for m in range(micro):
        got, earlier = dispatch(grid, cotangent[m, 0], earlier, *tables[m])
        incoming_rows.append(got)

    resid = tokens.astype(f32).reshape(count, width)
    scale_one = rms_scale(resid)
    normed = to_order((resid * scale_one * gain_one).astype(bf16))
    query, keyed, valued = [times(normed, w) for w in w_parts]
    scale_query = rms_scale(query)
    scale_key = rms_scale(keyed)
    split = lambda v: v.reshape(micro, rows, heads, HD)
    q_heads = rotate(split(query * scale_query * gain_query), cosine, sine).astype(bf16)
    k_all = rotate(split(keyed * scale_key * gain_key), cosine, sine).astype(bf16)
    v_all = split(valued).astype(bf16)
    allowed = (positions[None, None, :] <= positions[None, :, None]) | (
        positions[None, None, :] < prefix[:, 0][:, None, None]
    )
    scores = jnp.einsum("bqhd,bkhd->bhqk", q_heads, k_all, preferred_element_type=f32) * scaling
    scores = jnp.where(allowed[:, None], scores, masked_value)
    expo = jnp.exp(scores - jnp.max(scores, axis=-1, keepdims=True))
    probs = expo / jnp.sum(expo, axis=-1, keepdims=True)
    attended = jnp.einsum("bhqk,bkhd->bqhd", probs.astype(bf16), v_all, preferred_element_type=f32)
    attended = to_order(attended.reshape(count, width).astype(bf16))
    hidden_one = resid + times(attended, wout)
    scale_two = rms_scale(hidden_one)
    normed_two = (hidden_one * scale_two * gain_two).astype(bf16)
    router = jax.nn.softmax(jnp.dot(normed_two, wrouter, preferred_element_type=f32), axis=-1)

    blocks = ny * nx * nz * capacity
    h = width // 2
    grads = []
    d_rows_back = []
    outputs_back = []
    arrived = []
    for m in range(micro):
        got, earlier = dispatch(grid, normed_two[m * rows : (m + 1) * rows], earlier, *tables[m])
        arrived.append(got)
    times_t = lambda a, b: lax.dot_general(a, b, (((1,), (1,)), ((), ())), preferred_element_type=f32)
    across = lambda a, b: lax.dot_general(a, b, (((0,), (0,)), ((), ())), preferred_element_type=f32)
    at = jnp.arange(max(128, 2 * experts), dtype=jnp.int32)[None, :]
    d_steps = None
    out_steps = None
    for m in range(micro):
        row_in, g_in = arrived[m].reshape(blocks, width), incoming_rows[m].reshape(blocks, width)
        if m:
            row_in, g_in = after((row_in, g_in), out_rows)
        share = jax.nn.softmax(jnp.dot(row_in, wrouter, preferred_element_type=f32), axis=-1)
        share = jnp.sum(jnp.where(numbers[None, :] == me, share, 0.0), axis=-1, keepdims=True)
        gate_val = jnp.dot(row_in, w_gate[0], preferred_element_type=f32)
        up_val = jnp.dot(row_in, w_up[0], preferred_element_type=f32)
        back = jnp.dot(g_in, w_down[0], preferred_element_type=f32)
        if m:
            gate_val, up_val, back = after((gate_val, up_val, back), d_steps[1])
        sigmoid_val = jax.nn.sigmoid(gate_val)
        activated = gate_val * sigmoid_val
        hidden = (activated * up_val).astype(bf16)
        d_share = jnp.sum(hidden.astype(f32) * back, axis=-1, keepdims=True)
        d_hidden = back * share
        d_gate = (d_hidden * up_val * sigmoid_val * (1.0 + gate_val * (1.0 - sigmoid_val))).astype(bf16)
        d_up = (d_hidden * activated).astype(bf16)
        hidden_share = (hidden.astype(f32) * share).astype(bf16)
        if m:
            d_gate, d_up = after((d_gate, d_up), out_steps[1])
        d_rows = (times_t(d_gate, w_gate[0]) + times_t(d_up, w_up[0])).astype(bf16)
        high = d_share.astype(bf16)
        low = (d_share - high.astype(f32)).astype(bf16)
        extra = jnp.where(at == me, high, jnp.where(at == me + experts, low, 0.0)).astype(bf16)
        d_rows = jnp.concatenate([extra, d_rows], axis=1).reshape(ny, nx, nz, capacity, -1)
        hidden = after(hidden, d_rows, *([d_steps[2]] if m else []))
        d_steps = combine(grid, d_rows, h + extra.shape[1], None, *tables[m])
        d_rows_back.append(d_steps[0])
        out_rows = (times_t(hidden, w_down[0]) * share).astype(bf16)
        out_rows = out_rows.reshape(ny, nx, nz, capacity, width)
        last_out = out_steps
        out_steps = combine(grid, out_rows, h, d_steps[1] if m else None, *tables[m])
        outputs_back.append(out_steps[0])
        grads.append((row_in, d_gate, d_up, g_in, hidden_share))
    expert_sums = []
    grads = after(grads, out_rows, last_out[2])
    for step, (left, right) in enumerate(((3, 4), (0, 1), (0, 2))):
        if step:
            grads = after(grads, expert_sums[-1], (d_steps[1], d_steps[2])[step - 1])
        expert_sums.append(sum(across(part[left], part[right]) for part in grads))
    extra_width = d_rows_back[0].shape[1] - width
    output = hidden_one + jnp.concatenate(outputs_back, axis=0)
    half = w_gate.shape[2] // 2
    expert_grads = []
    for total in (expert_sums[1], expert_sums[2], expert_sums[0]):
        far = lax.dynamic_slice_in_dim(total, (1 - core) * half, half, axis=1)
        near_half = lax.dynamic_slice_in_dim(total, core * half, half, axis=1)
        expert_grads.append((near_half + swap(far.astype(bf16)).astype(f32))[None])

    incoming = cotangent.astype(f32).reshape(count, width)
    returned = jnp.concatenate(d_rows_back, axis=0)
    d_router = returned[:, :experts] + returned[:, experts : 2 * experts]
    d_logits = (router * (d_router - jnp.sum(router * d_router, axis=-1, keepdims=True))).astype(bf16)
    d_normed_two = returned[:, extra_width:] + jnp.einsum(
        "re,de->rd", d_logits, wrouter, preferred_element_type=f32
    )
    grad_route = jnp.einsum("rd,re->de", normed_two, d_logits, preferred_element_type=f32)
    d_norm_two, sum_two = norm_back(d_normed_two, hidden_one, scale_two, gain_two)
    d_hidden_one = incoming + d_norm_two
    d_branch = d_hidden_one.astype(bf16)
    grad_wout, sent, near_out, out_sums = reduce_product(grid, attended, d_branch)
    d_branch = after(d_branch, sent)

    d_mixed = jnp.concatenate(times_turned(d_branch, wout), axis=1)
    d_mixed = split(from_order(d_mixed.astype(bf16)).astype(bf16))
    d_probs = jnp.einsum("bqhd,bkhd->bhqk", d_mixed, v_all, preferred_element_type=f32)
    d_values = jnp.einsum("bhqk,bqhd->bkhd", probs.astype(bf16), d_mixed, preferred_element_type=f32)
    value_part = d_values.reshape(count, width).astype(bf16)
    grad_value, sent, near_value, value_sums = reduce_product(grid, normed, value_part)
    d_probs = after(d_probs, near_out, sent)
    d_scores = (
        probs * (d_probs - jnp.sum(probs * d_probs, axis=-1, keepdims=True)) * scaling
    ).astype(bf16)
    d_queries = jnp.einsum("bhqk,bkhd->bqhd", d_scores, k_all, preferred_element_type=f32)
    d_keys = jnp.einsum("bhqk,bqhd->bkhd", d_scores, q_heads, preferred_element_type=f32)
    d_queries, d_keys = after((d_queries, d_keys), near_value)
    d_query_normed = rotate(d_queries, cosine, -sine).reshape(count, width)
    d_key_normed = rotate(d_keys, cosine, -sine).reshape(count, width)
    d_query, sum_query = norm_back(d_query_normed, query, scale_query, gain_query)
    d_key, sum_key = norm_back(d_key_normed, keyed, scale_key, gain_key)
    query_part = d_query.astype(bf16)
    grad_query, sent, _, _ = reduce_product(grid, normed, query_part)
    key_part = after(d_key, sent, out_sums).astype(bf16)
    grad_key, sent, near_key, _ = reduce_product(grid, normed, key_part)
    d_parts = after([query_part, key_part, value_part], near_key, value_sums)
    d_normed = [
        sum(parts) for parts in zip(*[times_turned(part, w) for part, w in zip(d_parts, w_parts)])
    ]
    d_normed = jnp.concatenate(d_normed, axis=1)
    d_high = d_normed.astype(bf16)
    d_low = (d_normed - d_high.astype(f32)).astype(bf16)
    d_normed = from_order(d_high) + from_order(d_low)
    d_resid, sum_one = norm_back(d_normed, resid, scale_one, gain_one)
    input_grad = d_hidden_one + d_resid

    sums = jnp.concatenate([grad_route, jnp.stack([sum_one, sum_two, sum_query, sum_key], axis=1)], axis=1)
    sums = jnp.pad(sums, ((0, 0), (0, lanes - sums.shape[1])))
    parts = []
    for _ in range(3):
        parts.append(sums.astype(bf16))
        sums = sums - parts[-1].astype(f32)
    sums = sum(
        lax.dot_general(turn, part, (((0,), (0,)), ((), ())), preferred_element_type=f32)
        for part in parts
    )
    sums = reduce_small(grid, sums)
    grad_gains = [sums[:, experts + k] for k in range(4)]

    shape = (micro, 1, rows, width)
    return (
        output.reshape(shape),
        input_grad.reshape(shape),
        jnp.concatenate([grad_query, grad_key, grad_value], axis=1),
        grad_wout,
        sums[:, :experts],
        *grad_gains,
        *expert_grads,
    )


def solution(mesh):
    grid = Grid(mesh.shape["expert"])
    both = ("dp", "expert")
    tokens_spec = P(None, both, None, None)
    return jax.shard_map(
        lambda *args: shards(grid, *args),
        mesh=mesh,
        in_specs=(
            tokens_spec,
            tokens_spec,
            P(None, both),
            P(both, None),
            P(both, None),
            P(both, None),
            P(both),
            P(both),
            P(both),
            P(both),
            P("expert", None, None),
            P("expert", None, None),
            P("expert", None, None),
            tokens_spec,
        ),
        out_specs=(
            tokens_spec,
            tokens_spec,
            P(both, None),
            P(both, None),
            P(both, None),
            P(both),
            P(both),
            P(both),
            P(both),
            P("expert", None, "dp"),
            P("expert", None, "dp"),
            P("expert", None, "dp"),
        ),
        check_vma=False,
    )
```

```python
import jax
import jax.numpy as jnp
import numpy as np
from jax import lax
from jax.sharding import PartitionSpec as P

HD = 128
TOP = 8


epsilon = 1e-05
theta_base = 10000.0
masked_value = -1e30
bf16 = jnp.bfloat16
f32 = jnp.float32


def rms_scale(values):
    return lax.rsqrt(jnp.mean(values * values, axis=-1, keepdims=True) + epsilon)


def rope_tables(count, offset, width):
    halfway = width // 2
    inverse = theta_base ** (-(jnp.arange(halfway, dtype=f32) * 2.0) / width)
    places = offset + jnp.arange(count, dtype=f32)
    angles = places[:, None] * inverse[None, :]
    angles = jnp.concatenate([angles, angles], axis=1)
    return (jnp.cos(angles), jnp.sin(angles))


def rotate(values, cosine, sine):
    halfway = values.shape[-1] // 2
    turned = jnp.concatenate([-values[..., halfway:], values[..., :halfway]], axis=-1)
    return values * cosine[:, None, :] + turned * sine[:, None, :]


def norm_back(incoming, values, scaling, gain):
    weighted = incoming * gain
    inner = jnp.mean(weighted * values, axis=-1, keepdims=True)
    d_values = scaling * weighted - values * scaling * scaling * scaling * inner
    return (d_values, jnp.sum(incoming * values * scaling, axis=0))


def add_low(one, two):
    return (one.astype(f32) + two.astype(f32)).astype(one.dtype)


class Grid:
    def __init__(self, owners):
        self.owners = owners
        self.dims = {16: (4, 2, 2), 64: (4, 4, 4)}.get(owners, (owners, 1, 1))
        self.strides = (self.dims[1] * self.dims[2], self.dims[2], 1)

    def place(self):
        index = lax.axis_index("expert")
        return [index // s % n for s, n in zip(self.strides, self.dims)]

    def shift(self, values, axis, by):
        n, s = self.dims[axis], self.strides[axis]
        pairs = []
        for i in range(self.owners):
            c = i // s % n
            pairs.append((i, i + ((c + by) % n - c) * s))
        return lax.ppermute(values, "expert", pairs)

    def gather(self, values, axis):
        n = self.dims[axis]
        out = [values] + [None] * (n - 1)
        ahead = n // 2
        for k in range(1, ahead + 1):
            out[k] = self.shift(out[k - 1], axis, 1)
        for k in range(1, n - ahead):
            out[n - k] = self.shift(out[(n - k + 1) % n], axis, -1)
        return out

    def scatter(self, parts, axis, last=False, earlier=()):
        n = self.dims[axis]
        ahead = n // 2
        arrived = []
        if ahead:
            total = parts[ahead]
            for k in range(ahead - 1, -1, -1):
                total = self.shift(total, axis, -1)
                if k:
                    total = add_low(total, parts[k])
            arrived.append(total)
        if n - 1 - ahead:
            total = parts[ahead + 1]
            for k in range(ahead + 2, n + 1):
                total = self.shift(total, axis, 1)
                if k < n:
                    total = add_low(total, parts[k])
            arrived.append(total)
        total = after(parts[0], *earlier).astype(f32)
        for other in arrived:
            total = total + other.astype(f32)
        return total if last else total.astype(parts[0].dtype)


def after(values, *others):
    return lax.optimization_barrier((values, *others))[0] if others else values


def swap(values):
    return lax.ppermute(values, "dp", [(0, 1), (1, 0)])


def gather_weight(grid, shard, *earlier):
    half = shard.shape[0] // 2
    columns = shard.shape[1]
    pieces = []
    along = grid.gather(after(shard, *earlier), 0)
    for part, first, second in ((slice(0, half), 2, 1), (slice(half, None), 1, 2)):
        line = jnp.stack([piece[part] for piece in along])
        plane = jnp.stack(grid.gather(line, first))
        for piece in grid.gather(plane, second):
            pieces.append(piece.reshape(-1, columns))
    own = jnp.concatenate(pieces, axis=0)
    return (own, swap(own)), along[1:]


def times(values, weight):
    half = weight[0].shape[0]
    return sum(
        jnp.dot(values[:, k * half : (k + 1) * half], weight[k], preferred_element_type=f32)
        for k in range(2)
    )


def times_turned(values, weight):
    return [
        lax.dot_general(values, part, (((1,), (1,)), ((), ())), preferred_element_type=f32)
        for part in weight
    ]


def weight_order(grid, shard_rows):
    nz, ny, nx = grid.dims
    half = shard_rows // 2
    z, y, x = grid.place()
    core = lax.axis_index("dp")
    tables = []
    for dp_r in range(2):
        a = np.stack(np.meshgrid(np.arange(ny), np.arange(nx), np.arange(nz), np.arange(half), indexing="ij"), -1).reshape(-1, 4)
        b = np.stack(np.meshgrid(np.arange(nx), np.arange(ny), np.arange(nz), np.arange(half), indexing="ij"), -1).reshape(-1, 4)
        for color, (ry, rx, rz, i) in ((0, a.T), (1, (b.T[1], b.T[0], b.T[2], b.T[3]))):
            tables.append(np.stack([np.full_like(ry, dp_r), rz, ry, rx, i + color * half]))
    t = np.concatenate(tables, axis=1).astype(np.int32)
    where = ((core + 2 - t[0]) % 2) * grid.owners
    where = where + ((z + nz - t[1]) % nz) * grid.strides[0]
    where = where + ((y + ny - t[2]) % ny) * grid.strides[1] + (x + nx - t[3]) % nx
    return (where * shard_rows + t[4]).astype(jnp.int32)


def scatter_rows(grid, kept, *earlier):
    nz, ny, nx = grid.dims
    rows, columns = kept.shape
    out = []
    sums = []
    for part, first, second in ((kept[: rows // 2], 1, 2), (kept[rows // 2 :], 2, 1)):
        part = part.reshape(grid.dims[first], -1, columns)
        part = [part[k] for k in range(grid.dims[first])]
        part = grid.scatter(part, first, earlier=earlier)
        part = part.reshape(grid.dims[second], -1, columns)
        sums.append(part)
        part = grid.scatter([part[k] for k in range(grid.dims[second])], second)
        part = part.reshape(nz, -1, columns)
        out.append(grid.scatter([part[k] for k in range(nz)], 0, last=True))
    return jnp.concatenate(out, axis=0), sums


def partial_product(left, right):
    half = left.shape[1] // 2
    product = lambda a: lax.dot_general(a, right, (((0,), (0,)), ((), ())), preferred_element_type=f32)
    sent = product(left[:, half:]).astype(bf16)
    near = (product(left[:, :half]) + swap(sent).astype(f32)).astype(bf16)
    return sent, near


def reduce_small(grid, values):
    half = values.shape[0] // 2
    return scatter_rows(grid, values[:half] + swap(values[half:]))[0]


def pack(table, blocks):
    return lax.dot_general(
        table, blocks, (((3,), (2,)), ((0, 1), (0, 1))), preferred_element_type=f32
    ).astype(bf16)


def unpack(table, blocks):
    return lax.dot_general(
        table, blocks, (((2,), (2,)), ((0, 1), (0, 1))), preferred_element_type=f32
    ).astype(bf16)


def spread_plane(grid, along, *earlier):
    h = along[0].shape[1] // 2
    line = after(jnp.stack(along), *earlier)
    return jnp.stack(grid.gather(line[..., :h], 2)), jnp.stack(grid.gather(line[..., h:], 1))


def spread_packed(grid, planes, tables, *earlier):
    nz, ny, nx = grid.dims
    slots_own, slots_y, slots_x = after(tables, *earlier)
    left = [pack(slots_own[0], planes[0])]
    right = [pack(slots_own[:, 0], planes[1])]
    sent = [pack(slots_y[k - 1], planes[0]) for k in range(1, ny)]
    left += [grid.shift(rows, 1, k + 1) for k, rows in enumerate(sent)]
    more = [pack(slots_x[k - 1], planes[1]) for k in range(1, nx)]
    right += [grid.shift(rows, 2, k + 1) for k, rows in enumerate(more)]
    packed = jnp.concatenate([jnp.stack(left), jnp.stack(right, axis=1)], axis=-1)
    return packed, sent + more


def combine_first(grid, packed, h):
    nz, ny, nx = grid.dims
    left = [packed[0, ..., :h]]
    left += [grid.shift(packed[k, ..., :h], 1, -k) for k in range(1, ny)]
    right = [packed[:, 0, ..., h:]]
    right += [grid.shift(packed[:, k, ..., h:], 2, -k) for k in range(1, nx)]
    return left, right


def combine_plane(received, tables, *earlier):
    slots_own, slots_y, slots_x = after(tables, *earlier)
    left = unpack(jnp.concatenate([slots_own[0], *slots_y], axis=2), jnp.concatenate(received[0], axis=2))
    right = unpack(jnp.concatenate([slots_own[:, 0], *slots_x], axis=2), jnp.concatenate(received[1], axis=2))
    return left, right


def combine_line(grid, planes, *earlier):
    nz, ny, nx = grid.dims
    left = grid.scatter([planes[0][k] for k in range(nx)], 2, earlier=earlier)
    right = grid.scatter([planes[1][k] for k in range(ny)], 1, earlier=earlier)
    return jnp.concatenate([left, right], axis=-1)


def combine_last(grid, line):
    return grid.scatter([line[k] for k in range(grid.dims[0])], 0, last=True)


def shards(
    grid,
    tokens,
    routes,
    prefix,
    w_qkv,
    w_out,
    w_router,
    attn_gain,
    ffn_gain,
    query_gain,
    key_gain,
    w_gate,
    w_up,
    w_down,
    cotangent,
):
    micro = tokens.shape[0]
    rows = tokens.shape[2]
    width = tokens.shape[3]
    shard_rows = w_qkv.shape[0]
    experts = w_router.shape[1]
    nz, ny, nx = grid.dims
    heads = width // HD
    count = micro * rows
    capacity = max(2, rows * TOP * 9 // (experts * 8))
    scaling = HD ** (-0.5)
    cosine, sine = rope_tables(rows, 0.0, HD)
    positions = jnp.arange(rows, dtype=jnp.int32)
    numbers = jnp.arange(experts, dtype=jnp.int32)
    core = lax.axis_index("dp")
    me = lax.axis_index("expert")
    z, y, x = grid.place()

    lanes = rows
    small = jnp.concatenate(
        [w_router] + [gain[:, None] for gain in (attn_gain, ffn_gain, query_gain, key_gain)], axis=1
    )
    small = jnp.pad(small, ((0, 0), (0, lanes - small.shape[1])))
    member = jnp.any(routes[:, 0, None, :, :] == numbers[None, :, None, None], axis=-1)
    member = member.astype(bf16).reshape(micro * experts, rows)
    table = jnp.concatenate([small, member], axis=0)
    table = jnp.stack(grid.gather(table, 0))
    table = jnp.stack(grid.gather(table, 2))
    table = jnp.stack(grid.gather(table, 1))
    small = table[:, :, :, :shard_rows].reshape(-1, lanes)
    small = jnp.concatenate([small, swap(small)], axis=0)
    t = np.stack(
        np.meshgrid(*[np.arange(n) for n in (2, ny, nx, nz, shard_rows)], indexing="ij"), -1
    ).reshape(-1, 5).T.astype(np.int32)
    where = ((core + 2 - t[0]) % 2) * grid.owners + ((z + nz - t[3]) % nz) * grid.strides[0]
    where = where + ((y + ny - t[1]) % ny) * grid.strides[1] + (x + nx - t[2]) % nx
    where = where * shard_rows + t[4]
    features = jnp.arange(width, dtype=jnp.int32)
    spot = (features[:, None] == where[None, :]).astype(bf16)
    small = jnp.dot(spot, small, preferred_element_type=f32)
    wrouter = small[:, :experts].astype(bf16)
    gain_one, gain_two, gain_query, gain_key = [small[:, experts + k] for k in range(4)]
    member = table[:, :, :, shard_rows:].reshape(ny, nx, nz, micro, experts, rows)
    triangle = (positions[:, None] <= positions[None, :]).astype(bf16)
    ranks = jnp.dot(member, triangle, preferred_element_type=f32).astype(jnp.int32) - 1
    ranks = jnp.where(member > 0, ranks, -1)
    ranks = jnp.transpose(ranks, (4, 3, 0, 1, 2, 5))
    slot_numbers = jnp.arange(capacity, dtype=jnp.int32)
    expand = lambda r: (r[..., None, :] == slot_numbers[:, None]).astype(bf16)
    pick = lambda e: lax.dynamic_index_in_dim(ranks, e, 0, keepdims=False)
    near = lambda dy, dx: (z * ny + (y + dy) % ny) * nx + (x + dx) % nx
    slots_own = expand(pick(me))
    slots_y = [expand(pick(near(k, 0))[:, 0]) for k in range(1, ny)]
    slots_x = [expand(pick(near(0, k))[:, :, 0]) for k in range(1, nx)]
    tables = [
        (slots_own[m], [s[m] for s in slots_y], [s[m] for s in slots_x]) for m in range(micro)
    ]

    order = weight_order(grid, shard_rows)
    turn = (features[:, None] == order[None, :]).astype(bf16)
    to_order = lambda v: jnp.dot(v, turn, preferred_element_type=f32).astype(bf16)
    from_order = lambda v: lax.dot_general(
        v, turn, (((1,), (1,)), ((), ())), preferred_element_type=f32
    )

    w_parts = []
    earlier = [table]
    for w in [w_qkv[:, k * width : (k + 1) * width] for k in range(3)] + [w_out]:
        gathered, earlier = gather_weight(grid, w, *earlier)
        w_parts.append(gathered)
    wout = w_parts.pop()
    g_lines = []
    for m in range(micro):
        g_lines.append(grid.gather(after(cotangent[m, 0], *earlier), 0))
        earlier = g_lines[-1][1:]
    g_planes = [
        spread_plane(grid, line, (w_parts[2] if m == 0 else wout)[0]) for m, line in enumerate(g_lines)
    ]

    resid = tokens.astype(f32).reshape(count, width)
    scale_one = rms_scale(resid)
    normed = to_order((resid * scale_one * gain_one).astype(bf16))
    query, keyed, valued = [times(normed, w) for w in w_parts]
    scale_query = rms_scale(query)
    scale_key = rms_scale(keyed)
    split = lambda v: v.reshape(micro, rows, heads, HD)
    q_heads = rotate(split(query * scale_query * gain_query), cosine, sine).astype(bf16)
    k_all = rotate(split(keyed * scale_key * gain_key), cosine, sine).astype(bf16)
    v_all = split(valued).astype(bf16)
    allowed = (positions[None, None, :] <= positions[None, :, None]) | (
        positions[None, None, :] < prefix[:, 0][:, None, None]
    )
    scores = jnp.einsum("bqhd,bkhd->bhqk", q_heads, k_all, preferred_element_type=f32) * scaling
    scores = jnp.where(allowed[:, None], scores, masked_value)
    expo = jnp.exp(scores - jnp.max(scores, axis=-1, keepdims=True))
    probs = expo / jnp.sum(expo, axis=-1, keepdims=True)
    attended = jnp.einsum("bhqk,bkhd->bqhd", probs.astype(bf16), v_all, preferred_element_type=f32)
    attended = attended.reshape(count, width).astype(bf16)
    incoming_rows = [spread_packed(grid, g_planes[m], tables[m], attended)[0] for m in range(micro)]
    attended = to_order(attended)
    hidden_one = resid + times(attended, wout)
    scale_two = rms_scale(hidden_one)
    normed_two = (hidden_one * scale_two * gain_two).astype(bf16)
    router = jax.nn.softmax(jnp.dot(normed_two, wrouter, preferred_element_type=f32), axis=-1)

    blocks = ny * nx * nz * capacity
    h = width // 2
    grads = []
    arrived = []
    n_lines = []
    for m in range(micro):
        rows_m = normed_two[m * rows : (m + 1) * rows]
        n_lines.append(grid.gather(after(rows_m, *(n_lines[-1][1:] if m else [])), 0))
    sent = []
    for m in range(micro):
        planes = spread_plane(grid, n_lines[m], *sent)
        got, sent = spread_packed(grid, planes, tables[m])
        arrived.append(got)
    times_t = lambda a, b: lax.dot_general(a, b, (((1,), (1,)), ((), ())), preferred_element_type=f32)
    across = lambda a, b: lax.dot_general(a, b, (((0,), (0,)), ((), ())), preferred_element_type=f32)
    at = jnp.arange(max(128, 2 * experts), dtype=jnp.int32)[None, :]
    steps = []
    for m in range(micro):
        row_in, g_in = arrived[m].reshape(blocks, width), incoming_rows[m].reshape(blocks, width)
        if m:
            row_in, g_in = after((row_in, g_in), steps[-1]["out_rows"])
        share = jax.nn.softmax(jnp.dot(row_in, wrouter, preferred_element_type=f32), axis=-1)
        share = jnp.sum(jnp.where(numbers[None, :] == me, share, 0.0), axis=-1, keepdims=True)
        gate_val = jnp.dot(row_in, w_gate[0], preferred_element_type=f32)
        up_val = jnp.dot(row_in, w_up[0], preferred_element_type=f32)
        back = jnp.dot(g_in, w_down[0], preferred_element_type=f32)
        if m:
            before = steps[-1]
            before["d_plane"] = combine_plane(before["d_first"], tables[m - 1])
            share = after(share, *before["d_plane"])
        sigmoid_val = jax.nn.sigmoid(gate_val)
        activated = gate_val * sigmoid_val
        hidden = (activated * up_val).astype(bf16)
        d_share = jnp.sum(hidden.astype(f32) * back, axis=-1, keepdims=True)
        d_hidden = back * share
        d_gate = (d_hidden * up_val * sigmoid_val * (1.0 + gate_val * (1.0 - sigmoid_val))).astype(bf16)
        d_up = (d_hidden * activated).astype(bf16)
        hidden_share = (hidden.astype(f32) * share).astype(bf16)
        d_rows = (times_t(d_gate, w_gate[0]) + times_t(d_up, w_up[0])).astype(bf16)
        high = d_share.astype(bf16)
        low = (d_share - high.astype(f32)).astype(bf16)
        extra = jnp.where(at == me, high, jnp.where(at == me + experts, low, 0.0)).astype(bf16)
        d_rows = jnp.concatenate([extra, d_rows], axis=1).reshape(ny, nx, nz, capacity, -1)
        d_first = combine_first(grid, d_rows, h + extra.shape[1])
        hidden = after(hidden, d_rows)
        if m:
            before["d_line"] = combine_line(grid, before["d_plane"])
            hidden = after(hidden, before["d_line"])
        out_rows = (times_t(hidden, w_down[0]) * share).astype(bf16)
        out_rows = out_rows.reshape(ny, nx, nz, capacity, width)
        if m:
            before["out_plane"] = combine_plane(before["out_first"], tables[m - 1], d_rows)
        if m < micro - 1:
            out_first = combine_first(grid, out_rows, h)
        steps.append(dict(d_rows=d_rows, out_rows=out_rows, d_first=d_first, out_first=out_first))
        grads.append((row_in, d_gate, d_up, g_in, hidden_share))
    before, final = steps[-2], steps[-1]
    final["d_plane"] = combine_plane(final["d_first"], tables[-1])
    final["d_line"] = combine_line(grid, final["d_plane"])
    before["out_line"] = combine_line(grid, before["out_plane"], final["d_line"])
    out_first = combine_first(grid, after(final["out_rows"], *final["d_plane"]), h)
    expert_sums = []
    ties = [(final["out_rows"], *before["out_plane"]), final["d_plane"], (final["d_line"],)]
    for (left, right), tie in zip(((3, 4), (0, 1), (0, 2)), ties):
        grads = after(grads, *tie, *expert_sums[-1:])
        expert_sums.append(sum(across(part[left], part[right]) for part in grads))
    d_rows_back = [combine_last(grid, step["d_line"]) for step in steps]
    extra_width = d_rows_back[0].shape[1] - width
    incoming = cotangent.astype(f32).reshape(count, width)
    returned = jnp.concatenate(d_rows_back, axis=0)
    d_router = returned[:, :experts] + returned[:, experts : 2 * experts]
    d_logits = (router * (d_router - jnp.sum(router * d_router, axis=-1, keepdims=True))).astype(bf16)
    d_normed_two = returned[:, extra_width:] + jnp.einsum(
        "re,de->rd", d_logits, wrouter, preferred_element_type=f32
    )
    grad_route = jnp.einsum("rd,re->de", normed_two, d_logits, preferred_element_type=f32)
    d_norm_two, sum_two = norm_back(d_normed_two, hidden_one, scale_two, gain_two)
    d_hidden_one = incoming + d_norm_two
    d_branch = d_hidden_one.astype(bf16)
    sent, near_out = partial_product(attended, d_branch)
    d_branch = after(d_branch, sent)

    d_mixed = jnp.concatenate(times_turned(d_branch, wout), axis=1)
    d_mixed = split(from_order(d_mixed.astype(bf16)).astype(bf16))
    d_probs = jnp.einsum("bqhd,bkhd->bhqk", d_mixed, v_all, preferred_element_type=f32)
    d_values = jnp.einsum("bhqk,bqhd->bkhd", probs.astype(bf16), d_mixed, preferred_element_type=f32)
    value_part = d_values.reshape(count, width).astype(bf16)
    sent, near_value = partial_product(normed, value_part)
    inner = after(jnp.sum(probs * d_probs, axis=-1, keepdims=True), near_out, sent)
    d_scores = (probs * (d_probs - inner) * scaling).astype(bf16)
    final["out_plane"] = combine_plane(out_first, tables[-1], near_out)
    final["out_line"] = combine_line(grid, final["out_plane"], near_value)
    output = hidden_one + jnp.concatenate([combine_last(grid, step["out_line"]) for step in steps], axis=0)
    d_queries = jnp.einsum("bhqk,bkhd->bqhd", d_scores, k_all, preferred_element_type=f32)
    d_keys = jnp.einsum("bhqk,bqhd->bkhd", d_scores, q_heads, preferred_element_type=f32)
    back_sine = after(-sine, near_value)
    d_query_normed = rotate(d_queries, cosine, back_sine).reshape(count, width)
    d_key_normed = rotate(d_keys, cosine, back_sine).reshape(count, width)
    d_query, sum_query = norm_back(d_query_normed, query, scale_query, gain_query)
    query_part = d_query.astype(bf16)
    sent, near_query = partial_product(normed, query_part)
    d_key, sum_key = norm_back(d_key_normed, keyed, after(scale_key, sent), gain_key)
    key_part = d_key.astype(bf16)
    sent, near_key = partial_product(normed, key_part)
    grad_wout, _ = scatter_rows(grid, near_out, near_key)
    grad_value, _ = scatter_rows(grid, near_value, near_key)
    grad_query, query_sums = scatter_rows(grid, near_query)
    grad_key, key_sums = scatter_rows(grid, near_key)
    d_parts = after([query_part, key_part, value_part], near_key)
    d_normed = [
        sum(parts) for parts in zip(*[times_turned(part, w) for part, w in zip(d_parts, w_parts)])
    ]
    d_normed = jnp.concatenate(d_normed, axis=1)
    d_high = d_normed.astype(bf16)
    d_low = (d_normed - d_high.astype(f32)).astype(bf16)
    d_normed = from_order(d_high) + from_order(d_low)
    d_resid, sum_one = norm_back(d_normed, resid, scale_one, gain_one)
    input_grad = d_hidden_one + d_resid

    sums = jnp.concatenate([grad_route, jnp.stack([sum_one, sum_two, sum_query, sum_key], axis=1)], axis=1)
    sums = jnp.pad(sums, ((0, 0), (0, lanes - sums.shape[1])))
    parts = []
    for _ in range(3):
        parts.append(sums.astype(bf16))
        sums = sums - parts[-1].astype(f32)
    sums = sum(
        lax.dot_general(turn, part, (((0,), (0,)), ((), ())), preferred_element_type=f32)
        for part in parts
    )
    sums = reduce_small(grid, after(sums, *query_sums, *key_sums))
    grad_gains = [sums[:, experts + k] for k in range(4)]

    half = w_gate.shape[2] // 2
    side = after(core, near_key)
    expert_grads = []
    for total in (expert_sums[1], expert_sums[2], expert_sums[0]):
        far = lax.dynamic_slice_in_dim(total, (1 - side) * half, half, axis=1)
        near_half = lax.dynamic_slice_in_dim(total, side * half, half, axis=1)
        expert_grads.append((near_half + swap(far.astype(bf16)).astype(f32))[None])

    shape = (micro, 1, rows, width)
    return (
        output.reshape(shape),
        input_grad.reshape(shape),
        jnp.concatenate([grad_query, grad_key, grad_value], axis=1),
        grad_wout,
        sums[:, :experts],
        *grad_gains,
        *expert_grads,
    )


def solution(mesh):
    grid = Grid(mesh.shape["expert"])
    both = ("dp", "expert")
    tokens_spec = P(None, both, None, None)
    return jax.shard_map(
        lambda *args: shards(grid, *args),
        mesh=mesh,
        in_specs=(
            tokens_spec,
            tokens_spec,
            P(None, both),
            P(both, None),
            P(both, None),
            P(both, None),
            P(both),
            P(both),
            P(both),
            P(both),
            P("expert", None, None),
            P("expert", None, None),
            P("expert", None, None),
            tokens_spec,
        ),
        out_specs=(
            tokens_spec,
            tokens_spec,
            P(both, None),
            P(both, None),
            P(both, None),
            P(both),
            P(both),
            P(both),
            P(both),
            P("expert", None, "dp"),
            P("expert", None, "dp"),
            P("expert", None, "dp"),
        ),
        check_vma=False,
    )
```

```python
import jax
import jax.numpy as jnp
import numpy as np
from jax import lax
from jax.sharding import PartitionSpec as P

HD = 128
TOP = 8


epsilon = 1e-05
theta_base = 10000.0
masked_value = -1e30
bf16 = jnp.bfloat16
f32 = jnp.float32


def rms_scale(values):
    return lax.rsqrt(jnp.mean(values * values, axis=-1, keepdims=True) + epsilon)


def rope_tables(count, offset, width):
    halfway = width // 2
    inverse = theta_base ** (-(jnp.arange(halfway, dtype=f32) * 2.0) / width)
    places = offset + jnp.arange(count, dtype=f32)
    angles = places[:, None] * inverse[None, :]
    angles = jnp.concatenate([angles, angles], axis=1)
    return (jnp.cos(angles), jnp.sin(angles))


def rotate(values, cosine, sine):
    halfway = values.shape[-1] // 2
    turned = jnp.concatenate([-values[..., halfway:], values[..., :halfway]], axis=-1)
    return values * cosine[:, None, :] + turned * sine[:, None, :]


def norm_back(incoming, values, scaling, gain):
    weighted = incoming * gain
    inner = jnp.mean(weighted * values, axis=-1, keepdims=True)
    d_values = scaling * weighted - values * scaling * scaling * scaling * inner
    return (d_values, jnp.sum(incoming * values * scaling, axis=0))


def add_low(one, two):
    return (one.astype(f32) + two.astype(f32)).astype(one.dtype)


class Grid:
    def __init__(self, owners):
        self.owners = owners
        self.dims = {16: (4, 2, 2), 64: (4, 4, 4)}.get(owners, (owners, 1, 1))
        self.strides = (self.dims[1] * self.dims[2], self.dims[2], 1)

    def place(self):
        index = lax.axis_index("expert")
        return [index // s % n for s, n in zip(self.strides, self.dims)]

    def shift(self, values, axis, by):
        n, s = self.dims[axis], self.strides[axis]
        pairs = []
        for i in range(self.owners):
            c = i // s % n
            pairs.append((i, i + ((c + by) % n - c) * s))
        return lax.ppermute(values, "expert", pairs)

    def gather(self, values, axis):
        n = self.dims[axis]
        out = [values] + [None] * (n - 1)
        ahead = n // 2
        for k in range(1, ahead + 1):
            out[k] = self.shift(out[k - 1], axis, 1)
        for k in range(1, n - ahead):
            out[n - k] = self.shift(out[(n - k + 1) % n], axis, -1)
        return out

    def scatter(self, parts, axis, last=False, earlier=()):
        n = self.dims[axis]
        ahead = n // 2
        arrived = []
        if ahead:
            total = parts[ahead]
            for k in range(ahead - 1, -1, -1):
                total = self.shift(total, axis, -1)
                if k:
                    total = add_low(total, parts[k])
            arrived.append(total)
        if n - 1 - ahead:
            total = parts[ahead + 1]
            for k in range(ahead + 2, n + 1):
                total = self.shift(total, axis, 1)
                if k < n:
                    total = add_low(total, parts[k])
            arrived.append(total)
        total = after(parts[0], *earlier).astype(f32)
        for other in arrived:
            total = total + other.astype(f32)
        return total if last else total.astype(parts[0].dtype)


def after(values, *others):
    return lax.optimization_barrier((values, *others))[0] if others else values


def swap(values):
    return lax.ppermute(values, "dp", [(0, 1), (1, 0)])


def gather_weight(grid, shard, *earlier):
    half = shard.shape[0] // 2
    columns = shard.shape[1]
    pieces = []
    along = grid.gather(after(shard, *earlier), 0)
    for part, first, second in ((slice(0, half), 2, 1), (slice(half, None), 1, 2)):
        line = jnp.stack([piece[part] for piece in along])
        plane = jnp.stack(grid.gather(line, first))
        for piece in grid.gather(plane, second):
            pieces.append(piece.reshape(-1, columns))
    own = jnp.concatenate(pieces, axis=0)
    return (own, swap(own)), along[1:]


def times(values, weight):
    half = weight[0].shape[0]
    return sum(
        jnp.dot(values[:, k * half : (k + 1) * half], weight[k], preferred_element_type=f32)
        for k in range(2)
    )


def times_turned(values, weight):
    return [
        lax.dot_general(values, part, (((1,), (1,)), ((), ())), preferred_element_type=f32)
        for part in weight
    ]


def weight_order(grid, shard_rows):
    nz, ny, nx = grid.dims
    half = shard_rows // 2
    z, y, x = grid.place()
    core = lax.axis_index("dp")
    tables = []
    for dp_r in range(2):
        a = np.stack(np.meshgrid(np.arange(ny), np.arange(nx), np.arange(nz), np.arange(half), indexing="ij"), -1).reshape(-1, 4)
        b = np.stack(np.meshgrid(np.arange(nx), np.arange(ny), np.arange(nz), np.arange(half), indexing="ij"), -1).reshape(-1, 4)
        for color, (ry, rx, rz, i) in ((0, a.T), (1, (b.T[1], b.T[0], b.T[2], b.T[3]))):
            tables.append(np.stack([np.full_like(ry, dp_r), rz, ry, rx, i + color * half]))
    t = np.concatenate(tables, axis=1).astype(np.int32)
    where = ((core + 2 - t[0]) % 2) * grid.owners
    where = where + ((z + nz - t[1]) % nz) * grid.strides[0]
    where = where + ((y + ny - t[2]) % ny) * grid.strides[1] + (x + nx - t[3]) % nx
    return (where * shard_rows + t[4]).astype(jnp.int32)


def scatter_rows(grid, kept, *earlier):
    nz, ny, nx = grid.dims
    rows, columns = kept.shape
    out = []
    sums = []
    for part, first, second in ((kept[: rows // 2], 1, 2), (kept[rows // 2 :], 2, 1)):
        part = part.reshape(grid.dims[first], -1, columns)
        part = [part[k] for k in range(grid.dims[first])]
        part = grid.scatter(part, first, earlier=earlier)
        part = part.reshape(grid.dims[second], -1, columns)
        sums.append(part)
        part = grid.scatter([part[k] for k in range(grid.dims[second])], second)
        part = part.reshape(nz, -1, columns)
        out.append(grid.scatter([part[k] for k in range(nz)], 0, last=True))
    return jnp.concatenate(out, axis=0), sums


def partial_product(left, right):
    half = left.shape[1] // 2
    product = lambda a: lax.dot_general(a, right, (((0,), (0,)), ((), ())), preferred_element_type=f32)
    sent = product(left[:, half:]).astype(bf16)
    near = (product(left[:, :half]) + swap(sent).astype(f32)).astype(bf16)
    return sent, near


def reduce_small(grid, values):
    half = values.shape[0] // 2
    return scatter_rows(grid, values[:half] + swap(values[half:]))[0]


def pack(table, blocks):
    return lax.dot_general(
        table, blocks, (((3,), (2,)), ((0, 1), (0, 1))), preferred_element_type=f32
    ).astype(bf16)


def unpack(table, blocks):
    return lax.dot_general(
        table, blocks, (((2,), (2,)), ((0, 1), (0, 1))), preferred_element_type=f32
    ).astype(bf16)


def spread_plane(grid, along, *earlier):
    h = along[0].shape[1] // 2
    line = after(jnp.stack(along), *earlier)
    return jnp.stack(grid.gather(line[..., :h], 2)), jnp.stack(grid.gather(line[..., h:], 1))


def spread_packed(grid, planes, tables, *earlier):
    nz, ny, nx = grid.dims
    slots_own, slots_y, slots_x = after(tables, *earlier)
    left = [pack(slots_own[0], planes[0])]
    right = [pack(slots_own[:, 0], planes[1])]
    sent = [pack(slots_y[k - 1], planes[0]) for k in range(1, ny)]
    left += [grid.shift(rows, 1, k + 1) for k, rows in enumerate(sent)]
    more = [pack(slots_x[k - 1], planes[1]) for k in range(1, nx)]
    right += [grid.shift(rows, 2, k + 1) for k, rows in enumerate(more)]
    packed = jnp.concatenate([jnp.stack(left), jnp.stack(right, axis=1)], axis=-1)
    return packed, sent + more


def combine_first(grid, packed, h):
    nz, ny, nx = grid.dims
    left = [packed[0, ..., :h]]
    left += [grid.shift(packed[k, ..., :h], 1, -k) for k in range(1, ny)]
    right = [packed[:, 0, ..., h:]]
    right += [grid.shift(packed[:, k, ..., h:], 2, -k) for k in range(1, nx)]
    return left, right


def combine_plane(received, tables, *earlier):
    slots_own, slots_y, slots_x = after(tables, *earlier)
    left = unpack(jnp.concatenate([slots_own[0], *slots_y], axis=2), jnp.concatenate(received[0], axis=2))
    right = unpack(jnp.concatenate([slots_own[:, 0], *slots_x], axis=2), jnp.concatenate(received[1], axis=2))
    return left, right


def combine_line(grid, planes, *earlier):
    nz, ny, nx = grid.dims
    left = grid.scatter([planes[0][k] for k in range(nx)], 2, earlier=earlier)
    right = grid.scatter([planes[1][k] for k in range(ny)], 1, earlier=earlier)
    return jnp.concatenate([left, right], axis=-1)


def combine_last(grid, line):
    return grid.scatter([line[k] for k in range(grid.dims[0])], 0, last=True)


def shards(
    grid,
    tokens,
    routes,
    prefix,
    w_qkv,
    w_out,
    w_router,
    attn_gain,
    ffn_gain,
    query_gain,
    key_gain,
    w_gate,
    w_up,
    w_down,
    cotangent,
):
    micro = tokens.shape[0]
    rows = tokens.shape[2]
    width = tokens.shape[3]
    shard_rows = w_qkv.shape[0]
    experts = w_router.shape[1]
    nz, ny, nx = grid.dims
    heads = width // HD
    count = micro * rows
    capacity = max(2, rows * TOP * 9 // (experts * 8))
    scaling = HD ** (-0.5)
    cosine, sine = rope_tables(rows, 0.0, HD)
    positions = jnp.arange(rows, dtype=jnp.int32)
    numbers = jnp.arange(experts, dtype=jnp.int32)
    core = lax.axis_index("dp")
    me = lax.axis_index("expert")
    z, y, x = grid.place()

    lanes = rows
    small = jnp.concatenate(
        [w_router] + [gain[:, None] for gain in (attn_gain, ffn_gain, query_gain, key_gain)], axis=1
    )
    small = jnp.pad(small, ((0, 0), (0, lanes - small.shape[1])))
    member = jnp.any(routes[:, 0, None, :, :] == numbers[None, :, None, None], axis=-1)
    member = member.astype(bf16).reshape(micro * experts, rows)
    table = jnp.concatenate([small, member], axis=0)
    table = jnp.stack(grid.gather(table, 0))
    table = jnp.stack(grid.gather(table, 2))
    table = jnp.stack(grid.gather(table, 1))
    small = table[:, :, :, :shard_rows].reshape(-1, lanes)
    small = jnp.concatenate([small, swap(small)], axis=0)
    t = np.stack(
        np.meshgrid(*[np.arange(n) for n in (2, ny, nx, nz, shard_rows)], indexing="ij"), -1
    ).reshape(-1, 5).T.astype(np.int32)
    where = ((core + 2 - t[0]) % 2) * grid.owners + ((z + nz - t[3]) % nz) * grid.strides[0]
    where = where + ((y + ny - t[1]) % ny) * grid.strides[1] + (x + nx - t[2]) % nx
    where = where * shard_rows + t[4]
    features = jnp.arange(width, dtype=jnp.int32)
    spot = (features[:, None] == where[None, :]).astype(bf16)
    small = jnp.dot(spot, small, preferred_element_type=f32)
    wrouter = small[:, :experts].astype(bf16)
    gain_one, gain_two, gain_query, gain_key = [small[:, experts + k] for k in range(4)]
    member = table[:, :, :, shard_rows:].reshape(ny, nx, nz, micro, experts, rows)
    triangle = (positions[:, None] <= positions[None, :]).astype(bf16)
    ranks = jnp.dot(member, triangle, preferred_element_type=f32).astype(jnp.int32) - 1
    ranks = jnp.where(member > 0, ranks, -1)
    ranks = jnp.transpose(ranks, (4, 3, 0, 1, 2, 5))
    slot_numbers = jnp.arange(capacity, dtype=jnp.int32)
    expand = lambda r: (r[..., None, :] == slot_numbers[:, None]).astype(bf16)
    pick = lambda e: lax.dynamic_index_in_dim(ranks, e, 0, keepdims=False)
    near = lambda dy, dx: (z * ny + (y + dy) % ny) * nx + (x + dx) % nx
    slots_own = expand(pick(me))
    slots_y = [expand(pick(near(k, 0))[:, 0]) for k in range(1, ny)]
    slots_x = [expand(pick(near(0, k))[:, :, 0]) for k in range(1, nx)]
    tables = [
        (slots_own[m], [s[m] for s in slots_y], [s[m] for s in slots_x]) for m in range(micro)
    ]

    order = weight_order(grid, shard_rows)
    turn = (features[:, None] == order[None, :]).astype(bf16)
    to_order = lambda v: jnp.dot(v, turn, preferred_element_type=f32).astype(bf16)
    from_order = lambda v: lax.dot_general(
        v, turn, (((1,), (1,)), ((), ())), preferred_element_type=f32
    )

    w_parts = []
    earlier = [table]
    for w in [w_qkv[:, k * width : (k + 1) * width] for k in range(3)] + [w_out]:
        gathered, earlier = gather_weight(grid, w, *earlier)
        w_parts.append(gathered)
    wout = w_parts.pop()
    g_lines = []
    for m in range(micro):
        g_lines.append(grid.gather(after(cotangent[m, 0], *earlier), 0))
        earlier = g_lines[-1][1:]
    g_planes = [
        spread_plane(grid, line, (w_parts[2] if m == 0 else wout)[0]) for m, line in enumerate(g_lines)
    ]

    resid = tokens.astype(f32).reshape(count, width)
    scale_one = rms_scale(resid)
    normed = to_order((resid * scale_one * gain_one).astype(bf16))
    query, keyed, valued = [times(normed, w) for w in w_parts]
    scale_query = rms_scale(query)
    scale_key = rms_scale(keyed)
    split = lambda v: v.reshape(micro, rows, heads, HD)
    q_heads = rotate(split(query * scale_query * gain_query), cosine, sine).astype(bf16)
    k_all = rotate(split(keyed * scale_key * gain_key), cosine, sine).astype(bf16)
    v_all = split(valued).astype(bf16)
    allowed = (positions[None, None, :] <= positions[None, :, None]) | (
        positions[None, None, :] < prefix[:, 0][:, None, None]
    )
    scores = jnp.einsum("bqhd,bkhd->bhqk", q_heads, k_all, preferred_element_type=f32) * scaling
    scores = jnp.where(allowed[:, None], scores, masked_value)
    peak = jnp.max(scores, axis=-1, keepdims=True)
    expo = jnp.exp(scores - peak)
    probs = expo / jnp.sum(expo, axis=-1, keepdims=True)
    attended = jnp.einsum("bhqk,bkhd->bqhd", probs.astype(bf16), v_all, preferred_element_type=f32)
    attended = attended.reshape(count, width).astype(bf16)
    incoming_rows = [
        spread_packed(grid, g_planes[m], tables[m], attended if m else peak)[0] for m in range(micro)
    ]
    attended = to_order(attended)
    hidden_one = resid + times(attended, wout)
    scale_two = rms_scale(hidden_one)
    normed_two = (hidden_one * scale_two * gain_two).astype(bf16)
    router = jax.nn.softmax(jnp.dot(normed_two, wrouter, preferred_element_type=f32), axis=-1)

    blocks = ny * nx * nz * capacity
    h = width // 2
    grads = []
    arrived = []
    n_lines = []
    for m in range(micro):
        rows_m = normed_two[m * rows : (m + 1) * rows]
        n_lines.append(grid.gather(after(rows_m, *(n_lines[-1][1:] if m else [])), 0))
    sent = []
    for m in range(micro):
        planes = spread_plane(grid, n_lines[m], *sent)
        got, sent = spread_packed(grid, planes, tables[m])
        arrived.append(got)
    times_t = lambda a, b: lax.dot_general(a, b, (((1,), (1,)), ((), ())), preferred_element_type=f32)
    across = lambda a, b: lax.dot_general(a, b, (((0,), (0,)), ((), ())), preferred_element_type=f32)
    at = jnp.arange(max(128, 2 * experts), dtype=jnp.int32)[None, :]
    steps = []
    for m in range(micro):
        row_in, g_in = arrived[m].reshape(blocks, width), incoming_rows[m].reshape(blocks, width)
        if m:
            row_in, g_in = after((row_in, g_in), steps[-1]["out_rows"])
        share = jax.nn.softmax(jnp.dot(row_in, wrouter, preferred_element_type=f32), axis=-1)
        share = jnp.sum(jnp.where(numbers[None, :] == me, share, 0.0), axis=-1, keepdims=True)
        gate_val = jnp.dot(row_in, w_gate[0], preferred_element_type=f32)
        up_val = jnp.dot(row_in, w_up[0], preferred_element_type=f32)
        back = jnp.dot(g_in, w_down[0], preferred_element_type=f32)
        if m:
            before = steps[-1]
            before["d_plane"] = combine_plane(before["d_first"], tables[m - 1])
            before["out_first"] = combine_first(grid, after(before["out_rows"], *before["d_plane"]), h)
            share = after(share, *before["d_plane"])
        sigmoid_val = jax.nn.sigmoid(gate_val)
        activated = gate_val * sigmoid_val
        hidden = (activated * up_val).astype(bf16)
        d_share = jnp.sum(hidden.astype(f32) * back, axis=-1, keepdims=True)
        d_hidden = back * share
        d_gate = (d_hidden * up_val * sigmoid_val * (1.0 + gate_val * (1.0 - sigmoid_val))).astype(bf16)
        d_up = (d_hidden * activated).astype(bf16)
        hidden_share = (hidden.astype(f32) * share).astype(bf16)
        d_rows = (times_t(d_gate, w_gate[0]) + times_t(d_up, w_up[0])).astype(bf16)
        high = d_share.astype(bf16)
        low = (d_share - high.astype(f32)).astype(bf16)
        extra = jnp.where(at == me, high, jnp.where(at == me + experts, low, 0.0)).astype(bf16)
        d_rows = jnp.concatenate([extra, d_rows], axis=1).reshape(ny, nx, nz, capacity, -1)
        d_first = combine_first(grid, d_rows, h + extra.shape[1])
        hidden = after(hidden, d_rows)
        if m:
            before["d_line"] = combine_line(grid, before["d_plane"])
            hidden = after(hidden, before["d_line"])
        out_rows = (times_t(hidden, w_down[0]) * share).astype(bf16)
        out_rows = out_rows.reshape(ny, nx, nz, capacity, width)
        if m:
            before["out_plane"] = combine_plane(before["out_first"], tables[m - 1], d_rows)
        steps.append(dict(out_rows=out_rows, d_first=d_first))
        grads.append((row_in, d_gate, d_up, g_in, hidden_share))
    before, final = steps[-2], steps[-1]
    final["d_plane"] = combine_plane(final["d_first"], tables[-1])
    final["d_line"] = combine_line(grid, final["d_plane"])
    before["out_line"] = combine_line(grid, before["out_plane"], final["d_line"])
    out_first = combine_first(grid, after(final["out_rows"], *final["d_plane"]), h)
    expert_sums = []
    ties = [(final["out_rows"], *before["out_plane"]), final["d_plane"], (final["d_line"],)]
    for (left, right), tie in zip(((3, 4), (0, 1), (0, 2)), ties):
        grads = after(grads, *tie, *expert_sums[-1:])
        expert_sums.append(sum(across(part[left], part[right]) for part in grads))
    d_rows_back = [combine_last(grid, step["d_line"]) for step in steps]
    extra_width = d_rows_back[0].shape[1] - width
    incoming = cotangent.astype(f32).reshape(count, width)
    returned = jnp.concatenate(d_rows_back, axis=0)
    d_router = returned[:, :experts] + returned[:, experts : 2 * experts]
    d_logits = (router * (d_router - jnp.sum(router * d_router, axis=-1, keepdims=True))).astype(bf16)
    d_normed_two = returned[:, extra_width:] + jnp.einsum(
        "re,de->rd", d_logits, wrouter, preferred_element_type=f32
    )
    grad_route = jnp.einsum("rd,re->de", normed_two, d_logits, preferred_element_type=f32)
    d_norm_two, sum_two = norm_back(
        d_normed_two, hidden_one, after(scale_two, expert_sums[-1]), gain_two
    )
    d_hidden_one = incoming + d_norm_two
    d_branch = d_hidden_one.astype(bf16)
    sent, near_out = partial_product(attended, d_branch)
    d_branch = after(d_branch, sent)

    d_mixed = jnp.concatenate(times_turned(d_branch, wout), axis=1)
    d_mixed = split(from_order(d_mixed.astype(bf16)).astype(bf16))
    d_probs = jnp.einsum("bqhd,bkhd->bhqk", d_mixed, v_all, preferred_element_type=f32)
    d_values = jnp.einsum("bhqk,bqhd->bkhd", probs.astype(bf16), d_mixed, preferred_element_type=f32)
    value_part = d_values.reshape(count, width).astype(bf16)
    sent, near_value = partial_product(normed, value_part)
    inner = after(jnp.sum(probs * d_probs, axis=-1, keepdims=True), near_out, sent)
    d_scores = (probs * (d_probs - inner) * scaling).astype(bf16)
    d_queries = jnp.einsum("bhqk,bkhd->bqhd", d_scores, k_all, preferred_element_type=f32)
    d_keys = jnp.einsum("bhqk,bqhd->bkhd", d_scores, q_heads, preferred_element_type=f32)
    back_sine = after(-sine, near_value)
    d_query_normed = rotate(d_queries, cosine, back_sine).reshape(count, width)
    d_key_normed = rotate(d_keys, cosine, back_sine).reshape(count, width)
    d_query, sum_query = norm_back(d_query_normed, query, scale_query, gain_query)
    query_part = d_query.astype(bf16)
    sent, near_query = partial_product(normed, query_part)
    final["out_plane"] = combine_plane(out_first, tables[-1], sent)
    d_key, sum_key = norm_back(d_key_normed, keyed, after(scale_key, sent), gain_key)
    key_part = d_key.astype(bf16)
    sent, near_key = partial_product(normed, key_part)
    final["out_line"] = combine_line(grid, final["out_plane"], near_query, near_key)
    output = hidden_one + jnp.concatenate([combine_last(grid, step["out_line"]) for step in steps], axis=0)
    grad_wout, _ = scatter_rows(grid, near_out, near_query, near_key)
    grad_value, _ = scatter_rows(grid, near_value, near_query, near_key)
    grad_query, query_sums = scatter_rows(grid, near_query)
    grad_key, key_sums = scatter_rows(grid, near_key)
    d_parts = after([query_part, key_part, value_part], near_query, near_key)
    d_normed = [
        sum(parts) for parts in zip(*[times_turned(part, w) for part, w in zip(d_parts, w_parts)])
    ]
    d_normed = jnp.concatenate(d_normed, axis=1)
    d_high = d_normed.astype(bf16)
    d_low = (d_normed - d_high.astype(f32)).astype(bf16)
    d_normed = from_order(d_high) + from_order(d_low)
    d_resid, sum_one = norm_back(d_normed, resid, scale_one, gain_one)
    input_grad = d_hidden_one + d_resid

    half = w_gate.shape[2] // 2
    side = after(core, near_key)
    expert_grads = []
    for total in (expert_sums[1], expert_sums[2], expert_sums[0]):
        far = lax.dynamic_slice_in_dim(total, (1 - side) * half, half, axis=1)
        near_half = lax.dynamic_slice_in_dim(total, side * half, half, axis=1)
        expert_grads.append((near_half + swap(far.astype(bf16)).astype(f32))[None])

    sums = jnp.concatenate([grad_route, jnp.stack([sum_one, sum_two, sum_query, sum_key], axis=1)], axis=1)
    sums = jnp.pad(sums, ((0, 0), (0, lanes - sums.shape[1])))
    parts = []
    for _ in range(3):
        parts.append(sums.astype(bf16))
        sums = sums - parts[-1].astype(f32)
    sums = sum(
        lax.dot_general(turn, part, (((0,), (0,)), ((), ())), preferred_element_type=f32)
        for part in parts
    )
    sums = reduce_small(grid, after(sums, *query_sums, *key_sums, *expert_grads))
    grad_gains = [sums[:, experts + k] for k in range(4)]

    shape = (micro, 1, rows, width)
    return (
        output.reshape(shape),
        input_grad.reshape(shape),
        jnp.concatenate([grad_query, grad_key, grad_value], axis=1),
        grad_wout,
        sums[:, :experts],
        *grad_gains,
        *expert_grads,
    )


def solution(mesh):
    grid = Grid(mesh.shape["expert"])
    both = ("dp", "expert")
    tokens_spec = P(None, both, None, None)
    return jax.shard_map(
        lambda *args: shards(grid, *args),
        mesh=mesh,
        in_specs=(
            tokens_spec,
            tokens_spec,
            P(None, both),
            P(both, None),
            P(both, None),
            P(both, None),
            P(both),
            P(both),
            P(both),
            P(both),
            P("expert", None, None),
            P("expert", None, None),
            P("expert", None, None),
            tokens_spec,
        ),
        out_specs=(
            tokens_spec,
            tokens_spec,
            P(both, None),
            P(both, None),
            P(both, None),
            P(both),
            P(both),
            P(both),
            P(both),
            P("expert", None, "dp"),
            P("expert", None, "dp"),
            P("expert", None, "dp"),
        ),
        check_vma=False,
    )
```

```python
import jax
import jax.numpy as jnp
import numpy as np
from jax import lax
from jax.sharding import PartitionSpec as P

HD = 128
TOP = 8


epsilon = 1e-05
theta_base = 10000.0
masked_value = -1e30
bf16 = jnp.bfloat16
f32 = jnp.float32


def rms_scale(values):
    return lax.rsqrt(jnp.mean(values * values, axis=-1, keepdims=True) + epsilon)


def rope_tables(count, offset, width):
    halfway = width // 2
    inverse = theta_base ** (-(jnp.arange(halfway, dtype=f32) * 2.0) / width)
    places = offset + jnp.arange(count, dtype=f32)
    angles = places[:, None] * inverse[None, :]
    angles = jnp.concatenate([angles, angles], axis=1)
    return (jnp.cos(angles), jnp.sin(angles))


def rotate(values, cosine, sine):
    halfway = values.shape[-1] // 2
    turned = jnp.concatenate([-values[..., halfway:], values[..., :halfway]], axis=-1)
    return values * cosine[:, None, :] + turned * sine[:, None, :]


def norm_back(incoming, values, scaling, gain):
    weighted = incoming * gain
    inner = jnp.mean(weighted * values, axis=-1, keepdims=True)
    d_values = scaling * weighted - values * scaling * scaling * scaling * inner
    return (d_values, jnp.sum(incoming * values * scaling, axis=0))


def add_low(one, two):
    return (one.astype(f32) + two.astype(f32)).astype(one.dtype)


class Grid:
    def __init__(self, owners):
        self.owners = owners
        self.dims = {16: (4, 2, 2), 64: (4, 4, 4)}.get(owners, (owners, 1, 1))
        self.strides = (self.dims[1] * self.dims[2], self.dims[2], 1)

    def place(self):
        index = lax.axis_index("expert")
        return [index // s % n for s, n in zip(self.strides, self.dims)]

    def shift(self, values, axis, by):
        n, s = self.dims[axis], self.strides[axis]
        pairs = []
        for i in range(self.owners):
            c = i // s % n
            pairs.append((i, i + ((c + by) % n - c) * s))
        return lax.ppermute(values, "expert", pairs)

    def gather(self, values, axis):
        n = self.dims[axis]
        out = [values] + [None] * (n - 1)
        ahead = n // 2
        for k in range(1, ahead + 1):
            out[k] = self.shift(out[k - 1], axis, 1)
        for k in range(1, n - ahead):
            out[n - k] = self.shift(out[(n - k + 1) % n], axis, -1)
        return out

    def scatter(self, parts, axis, last=False, earlier=()):
        n = self.dims[axis]
        ahead = n // 2
        arrived = []
        if ahead:
            total = parts[ahead]
            for k in range(ahead - 1, -1, -1):
                total = self.shift(total, axis, -1)
                if k:
                    total = add_low(total, parts[k])
            arrived.append(total)
        if n - 1 - ahead:
            total = parts[ahead + 1]
            for k in range(ahead + 2, n + 1):
                total = self.shift(total, axis, 1)
                if k < n:
                    total = add_low(total, parts[k])
            arrived.append(total)
        total = after(parts[0], *earlier).astype(f32)
        for other in arrived:
            total = total + other.astype(f32)
        return total if last else total.astype(parts[0].dtype)


def after(values, *others):
    return lax.optimization_barrier((values, *others))[0] if others else values


def swap(values):
    return lax.ppermute(values, "dp", [(0, 1), (1, 0)])


def gather_weight(grid, shard, *earlier):
    half = shard.shape[0] // 2
    columns = shard.shape[1]
    pieces = []
    along = grid.gather(after(shard, *earlier), 0)
    for part, first, second in ((slice(0, half), 2, 1), (slice(half, None), 1, 2)):
        line = jnp.stack([piece[part] for piece in along])
        plane = jnp.stack(grid.gather(line, first))
        for piece in grid.gather(plane, second):
            pieces.append(piece.reshape(-1, columns))
    own = jnp.concatenate(pieces, axis=0)
    return (own, swap(own)), along[1:]


def times(values, weight):
    half = weight[0].shape[0]
    return sum(
        jnp.dot(values[:, k * half : (k + 1) * half], weight[k], preferred_element_type=f32)
        for k in range(2)
    )


def times_turned(values, weight):
    return [
        lax.dot_general(values, part, (((1,), (1,)), ((), ())), preferred_element_type=f32)
        for part in weight
    ]


def weight_order(grid, shard_rows):
    nz, ny, nx = grid.dims
    half = shard_rows // 2
    z, y, x = grid.place()
    core = lax.axis_index("dp")
    tables = []
    for dp_r in range(2):
        a = np.stack(np.meshgrid(np.arange(ny), np.arange(nx), np.arange(nz), np.arange(half), indexing="ij"), -1).reshape(-1, 4)
        b = np.stack(np.meshgrid(np.arange(nx), np.arange(ny), np.arange(nz), np.arange(half), indexing="ij"), -1).reshape(-1, 4)
        for color, (ry, rx, rz, i) in ((0, a.T), (1, (b.T[1], b.T[0], b.T[2], b.T[3]))):
            tables.append(np.stack([np.full_like(ry, dp_r), rz, ry, rx, i + color * half]))
    t = np.concatenate(tables, axis=1).astype(np.int32)
    where = ((core + 2 - t[0]) % 2) * grid.owners
    where = where + ((z + nz - t[1]) % nz) * grid.strides[0]
    where = where + ((y + ny - t[2]) % ny) * grid.strides[1] + (x + nx - t[3]) % nx
    return (where * shard_rows + t[4]).astype(jnp.int32)


def scatter_rows(grid, kept, *earlier, second=()):
    nz, ny, nx = grid.dims
    rows, columns = kept.shape
    out = []
    sums = []
    for part, first, after_it in ((kept[: rows // 2], 1, 2), (kept[rows // 2 :], 2, 1)):
        part = part.reshape(grid.dims[first], -1, columns)
        part = [part[k] for k in range(grid.dims[first])]
        part = grid.scatter(part, first, earlier=earlier)
        part = part.reshape(grid.dims[after_it], -1, columns)
        sums.append(part)
        part = grid.scatter([part[k] for k in range(grid.dims[after_it])], after_it, earlier=second)
        part = part.reshape(nz, -1, columns)
        out.append(grid.scatter([part[k] for k in range(nz)], 0, last=True))
    return jnp.concatenate(out, axis=0), sums


def partial_product(left, right):
    half = left.shape[1] // 2
    product = lambda a: lax.dot_general(a, right, (((0,), (0,)), ((), ())), preferred_element_type=f32)
    sent = product(left[:, half:]).astype(bf16)
    near = (product(left[:, :half]) + swap(sent).astype(f32)).astype(bf16)
    return sent, near


def reduce_small(grid, values):
    half = values.shape[0] // 2
    return scatter_rows(grid, values[:half] + swap(values[half:]))[0]


def pack(table, blocks):
    return lax.dot_general(
        table, blocks, (((3,), (2,)), ((0, 1), (0, 1))), preferred_element_type=f32
    ).astype(bf16)


def unpack(table, blocks):
    return lax.dot_general(
        table, blocks, (((2,), (2,)), ((0, 1), (0, 1))), preferred_element_type=f32
    ).astype(bf16)


def spread_plane(grid, along, *earlier):
    h = along[0].shape[1] // 2
    line = jnp.stack(after(along, *earlier))
    return grid.gather(line[..., :h], 2), grid.gather(line[..., h:], 1)


def spread_packed(grid, planes, tables, *earlier):
    nz, ny, nx = grid.dims
    planes, (slots_own, slots_y, slots_x) = after((planes, tables), *earlier)
    planes = [jnp.stack(plane) for plane in planes]
    left = [pack(slots_own[0], planes[0])]
    right = [pack(slots_own[:, 0], planes[1])]
    sent = [pack(slots_y[k - 1], planes[0]) for k in range(1, ny)]
    left += [grid.shift(rows, 1, k + 1) for k, rows in enumerate(sent)]
    more = [pack(slots_x[k - 1], planes[1]) for k in range(1, nx)]
    right += [grid.shift(rows, 2, k + 1) for k, rows in enumerate(more)]
    packed = jnp.concatenate([jnp.stack(left), jnp.stack(right, axis=1)], axis=-1)
    return packed, sent + more


def combine_first(grid, packed, h):
    nz, ny, nx = grid.dims
    left = [packed[0, ..., :h]]
    left += [grid.shift(packed[k, ..., :h], 1, -k) for k in range(1, ny)]
    right = [packed[:, 0, ..., h:]]
    right += [grid.shift(packed[:, k, ..., h:], 2, -k) for k in range(1, nx)]
    return left, right


def combine_plane(received, tables, *earlier):
    received, (slots_own, slots_y, slots_x) = after((received, tables), *earlier)
    left = unpack(jnp.concatenate([slots_own[0], *slots_y], axis=2), jnp.concatenate(received[0], axis=2))
    right = unpack(jnp.concatenate([slots_own[:, 0], *slots_x], axis=2), jnp.concatenate(received[1], axis=2))
    return left, right


def combine_line(grid, planes, *earlier):
    nz, ny, nx = grid.dims
    left = grid.scatter([planes[0][k] for k in range(nx)], 2, earlier=earlier)
    right = grid.scatter([planes[1][k] for k in range(ny)], 1, earlier=earlier)
    return jnp.concatenate([left, right], axis=-1)


def combine_last(grid, line):
    return grid.scatter([line[k] for k in range(grid.dims[0])], 0, last=True)


def shards(
    grid,
    tokens,
    routes,
    prefix,
    w_qkv,
    w_out,
    w_router,
    attn_gain,
    ffn_gain,
    query_gain,
    key_gain,
    w_gate,
    w_up,
    w_down,
    cotangent,
):
    micro = tokens.shape[0]
    rows = tokens.shape[2]
    width = tokens.shape[3]
    shard_rows = w_qkv.shape[0]
    experts = w_router.shape[1]
    nz, ny, nx = grid.dims
    heads = width // HD
    count = micro * rows
    capacity = max(2, rows * TOP * 9 // (experts * 8))
    scaling = HD ** (-0.5)
    cosine, sine = rope_tables(rows, 0.0, HD)
    positions = jnp.arange(rows, dtype=jnp.int32)
    numbers = jnp.arange(experts, dtype=jnp.int32)
    core = lax.axis_index("dp")
    me = lax.axis_index("expert")
    z, y, x = grid.place()

    lanes = rows
    small = jnp.concatenate(
        [w_router] + [gain[:, None] for gain in (attn_gain, ffn_gain, query_gain, key_gain)], axis=1
    )
    small = jnp.pad(small, ((0, 0), (0, lanes - small.shape[1])))
    member = jnp.any(routes[:, 0, None, :, :] == numbers[None, :, None, None], axis=-1)
    member = member.astype(bf16).reshape(micro * experts, rows)
    table = jnp.concatenate([small, member], axis=0)
    table = jnp.stack(grid.gather(table, 0))
    table = jnp.stack(grid.gather(table, 2))
    table = jnp.stack(grid.gather(table, 1))
    small = table[:, :, :, :shard_rows].reshape(-1, lanes)
    small = jnp.concatenate([small, swap(small)], axis=0)
    t = np.stack(
        np.meshgrid(*[np.arange(n) for n in (2, ny, nx, nz, shard_rows)], indexing="ij"), -1
    ).reshape(-1, 5).T.astype(np.int32)
    where = ((core + 2 - t[0]) % 2) * grid.owners + ((z + nz - t[3]) % nz) * grid.strides[0]
    where = where + ((y + ny - t[1]) % ny) * grid.strides[1] + (x + nx - t[2]) % nx
    where = where * shard_rows + t[4]
    features = jnp.arange(width, dtype=jnp.int32)
    spot = (features[:, None] == where[None, :]).astype(bf16)
    small = jnp.dot(spot, small, preferred_element_type=f32)
    wrouter = small[:, :experts].astype(bf16)
    gain_one, gain_two, gain_query, gain_key = [small[:, experts + k] for k in range(4)]
    member = table[:, :, :, shard_rows:].reshape(ny, nx, nz, micro, experts, rows)
    triangle = (positions[:, None] <= positions[None, :]).astype(bf16)
    ranks = jnp.dot(member, triangle, preferred_element_type=f32).astype(jnp.int32) - 1
    ranks = jnp.where(member > 0, ranks, -1)
    ranks = jnp.transpose(ranks, (4, 3, 0, 1, 2, 5))
    slot_numbers = jnp.arange(capacity, dtype=jnp.int32)
    expand = lambda r: (r[..., None, :] == slot_numbers[:, None]).astype(bf16)
    pick = lambda e: lax.dynamic_index_in_dim(ranks, e, 0, keepdims=False)
    near = lambda dy, dx: (z * ny + (y + dy) % ny) * nx + (x + dx) % nx
    slots_own = expand(pick(me))
    slots_y = [expand(pick(near(k, 0))[:, 0]) for k in range(1, ny)]
    slots_x = [expand(pick(near(0, k))[:, :, 0]) for k in range(1, nx)]
    tables = [
        (slots_own[m], [s[m] for s in slots_y], [s[m] for s in slots_x]) for m in range(micro)
    ]

    order = weight_order(grid, shard_rows)
    turn = (features[:, None] == order[None, :]).astype(bf16)
    to_order = lambda v: jnp.dot(v, turn, preferred_element_type=f32).astype(bf16)
    from_order = lambda v: lax.dot_general(
        v, turn, (((1,), (1,)), ((), ())), preferred_element_type=f32
    )

    w_parts = []
    earlier = [table]
    for w in [w_qkv[:, k * width : (k + 1) * width] for k in range(3)] + [w_out]:
        gathered, earlier = gather_weight(grid, w, *earlier)
        w_parts.append(gathered)
    wout = w_parts.pop()
    g_lines = []
    for m in range(micro):
        g_lines.append(grid.gather(after(cotangent[m, 0], *earlier), 0))
        earlier = g_lines[-1][1:]
    g_planes = [
        spread_plane(grid, line, (w_parts[2] if m == 0 else wout)[0]) for m, line in enumerate(g_lines)
    ]

    resid = tokens.astype(f32).reshape(count, width)
    scale_one = rms_scale(resid)
    normed = to_order((resid * scale_one * gain_one).astype(bf16))
    query, keyed, valued = [times(normed, w) for w in w_parts]
    scale_query = rms_scale(query)
    scale_key = rms_scale(keyed)
    split = lambda v: v.reshape(micro, rows, heads, HD)
    q_heads = rotate(split(query * scale_query * gain_query), cosine, sine).astype(bf16)
    k_all = rotate(split(keyed * scale_key * gain_key), cosine, sine).astype(bf16)
    v_all = split(valued).astype(bf16)
    allowed = (positions[None, None, :] <= positions[None, :, None]) | (
        positions[None, None, :] < prefix[:, 0][:, None, None]
    )
    scores = jnp.einsum("bqhd,bkhd->bhqk", q_heads, k_all, preferred_element_type=f32) * scaling
    scores = jnp.where(allowed[:, None], scores, masked_value)
    peak = jnp.max(scores, axis=-1, keepdims=True)
    expo = jnp.exp(scores - peak)
    probs = expo / jnp.sum(expo, axis=-1, keepdims=True)
    attended = jnp.einsum("bhqk,bkhd->bqhd", probs.astype(bf16), v_all, preferred_element_type=f32)
    attended = attended.reshape(count, width).astype(bf16)
    incoming_rows = [
        spread_packed(grid, g_planes[m], tables[m], attended if m else peak)[0] for m in range(micro)
    ]
    attended = to_order(attended)
    hidden_one = resid + times(attended, wout)
    scale_two = rms_scale(hidden_one)
    normed_two = (hidden_one * scale_two * gain_two).astype(bf16)
    router = jax.nn.softmax(jnp.dot(normed_two, wrouter, preferred_element_type=f32), axis=-1)

    blocks = ny * nx * nz * capacity
    h = width // 2
    grads = []
    arrived = []
    n_lines = []
    for m in range(micro):
        rows_m = normed_two[m * rows : (m + 1) * rows]
        n_lines.append(grid.gather(after(rows_m, *(n_lines[-1][1:] if m else [])), 0))
    sent = []
    for m in range(micro):
        planes = spread_plane(grid, n_lines[m], *sent)
        got, sent = spread_packed(grid, planes, tables[m])
        arrived.append(got)
    times_t = lambda a, b: lax.dot_general(a, b, (((1,), (1,)), ((), ())), preferred_element_type=f32)
    across = lambda a, b: lax.dot_general(a, b, (((0,), (0,)), ((), ())), preferred_element_type=f32)
    at = jnp.arange(max(128, 2 * experts), dtype=jnp.int32)[None, :]
    steps = []
    for m in range(micro):
        row_in, g_in = arrived[m].reshape(blocks, width), incoming_rows[m].reshape(blocks, width)
        if m:
            row_in, g_in = after((row_in, g_in), steps[-1]["out_rows"])
        share = jax.nn.softmax(jnp.dot(row_in, wrouter, preferred_element_type=f32), axis=-1)
        share = jnp.sum(jnp.where(numbers[None, :] == me, share, 0.0), axis=-1, keepdims=True)
        gate_val = jnp.dot(row_in, w_gate[0], preferred_element_type=f32)
        up_val = jnp.dot(row_in, w_up[0], preferred_element_type=f32)
        back = jnp.dot(g_in, w_down[0], preferred_element_type=f32)
        if m:
            before = steps[-1]
            before["d_plane"] = combine_plane(before["d_first"], tables[m - 1])
            before["out_first"] = combine_first(grid, after(before["out_rows"], *before["d_plane"]), h)
            share = after(share, *before["d_plane"])
        sigmoid_val = jax.nn.sigmoid(gate_val)
        activated = gate_val * sigmoid_val
        hidden = (activated * up_val).astype(bf16)
        d_share = jnp.sum(hidden.astype(f32) * back, axis=-1, keepdims=True)
        d_hidden = back * share
        d_gate = (d_hidden * up_val * sigmoid_val * (1.0 + gate_val * (1.0 - sigmoid_val))).astype(bf16)
        d_up = (d_hidden * activated).astype(bf16)
        hidden_share = (hidden.astype(f32) * share).astype(bf16)
        d_rows = (times_t(d_gate, w_gate[0]) + times_t(d_up, w_up[0])).astype(bf16)
        high = d_share.astype(bf16)
        low = (d_share - high.astype(f32)).astype(bf16)
        extra = jnp.where(at == me, high, jnp.where(at == me + experts, low, 0.0)).astype(bf16)
        d_rows = jnp.concatenate([extra, d_rows], axis=1).reshape(ny, nx, nz, capacity, -1)
        d_first = combine_first(grid, d_rows, h + extra.shape[1])
        hidden = after(hidden, d_rows)
        if m:
            before["d_line"] = combine_line(grid, before["d_plane"])
            hidden = after(hidden, before["d_line"])
        out_rows = (times_t(hidden, w_down[0]) * share).astype(bf16)
        out_rows = out_rows.reshape(ny, nx, nz, capacity, width)
        steps.append(dict(out_rows=out_rows, d_first=d_first))
        grads.append((row_in, d_gate, d_up, g_in, hidden_share))
    before, final = steps[-2], steps[-1]
    final["d_plane"] = combine_plane(final["d_first"], tables[-1])
    final["d_line"] = combine_line(grid, final["d_plane"])
    before["out_plane"] = combine_plane(before["out_first"], tables[-2], *final["d_plane"])
    out_first = combine_first(grid, after(final["out_rows"], *final["d_plane"]), h)
    expert_sums = []
    ties = [(final["out_rows"],), final["d_plane"], (final["d_line"],)]
    for (left, right), tie in zip(((3, 4), (0, 1), (0, 2)), ties):
        grads = after(grads, *tie, *expert_sums[-1:])
        expert_sums.append(sum(across(part[left], part[right]) for part in grads))
    d_rows_back = [combine_last(grid, step["d_line"]) for step in steps]
    extra_width = d_rows_back[0].shape[1] - width
    incoming = cotangent.astype(f32).reshape(count, width)
    returned = jnp.concatenate(d_rows_back, axis=0)
    d_router = returned[:, :experts] + returned[:, experts : 2 * experts]
    d_logits = (router * (d_router - jnp.sum(router * d_router, axis=-1, keepdims=True))).astype(bf16)
    d_normed_two = returned[:, extra_width:] + jnp.einsum(
        "re,de->rd", d_logits, wrouter, preferred_element_type=f32
    )
    grad_route = jnp.einsum("rd,re->de", normed_two, d_logits, preferred_element_type=f32)
    d_norm_two, sum_two = norm_back(
        d_normed_two, hidden_one, after(scale_two, expert_sums[-1]), gain_two
    )
    d_hidden_one = incoming + d_norm_two
    d_branch = d_hidden_one.astype(bf16)
    sent, near_out = partial_product(attended, d_branch)
    d_branch = after(d_branch, sent)

    d_mixed = jnp.concatenate(times_turned(d_branch, wout), axis=1)
    d_mixed = split(from_order(d_mixed.astype(bf16)).astype(bf16))
    d_probs = jnp.einsum("bqhd,bkhd->bhqk", d_mixed, v_all, preferred_element_type=f32)
    d_values = jnp.einsum("bhqk,bqhd->bkhd", probs.astype(bf16), d_mixed, preferred_element_type=f32)
    value_part = d_values.reshape(count, width).astype(bf16)
    sent, near_value = partial_product(normed, value_part)
    inner = after(jnp.sum(probs * d_probs, axis=-1, keepdims=True), near_out, sent)
    d_scores = (probs * (d_probs - inner) * scaling).astype(bf16)
    d_queries = jnp.einsum("bhqk,bkhd->bqhd", d_scores, k_all, preferred_element_type=f32)
    d_keys = jnp.einsum("bhqk,bqhd->bkhd", d_scores, q_heads, preferred_element_type=f32)
    before["out_line"] = combine_line(grid, before["out_plane"], near_value)
    back_sine = after(-sine, near_value)
    d_query_normed = rotate(d_queries, cosine, back_sine).reshape(count, width)
    d_key_normed = rotate(d_keys, cosine, back_sine).reshape(count, width)
    d_query, sum_query = norm_back(d_query_normed, query, scale_query, gain_query)
    query_part = d_query.astype(bf16)
    sent, near_query = partial_product(normed, query_part)
    d_key, sum_key = norm_back(d_key_normed, keyed, after(scale_key, sent), gain_key)
    key_part = d_key.astype(bf16)
    sent, near_key = partial_product(normed, key_part)
    half = w_gate.shape[2] // 2
    side = after(core, near_key)
    expert_grads = []
    for total in (expert_sums[1], expert_sums[2], expert_sums[0]):
        far = lax.dynamic_slice_in_dim(total, (1 - side) * half, half, axis=1)
        near_half = lax.dynamic_slice_in_dim(total, side * half, half, axis=1)
        expert_grads.append((near_half + swap(far.astype(bf16)).astype(f32))[None])
    final["out_plane"] = combine_plane(out_first, tables[-1], near_query, near_key)
    grad_query, query_sums = scatter_rows(grid, near_query, second=expert_grads)
    grad_key, key_sums = scatter_rows(grid, near_key, second=expert_grads)
    both = [*query_sums, *key_sums]
    grad_wout, out_sums = scatter_rows(grid, near_out, near_query, near_key, second=both)
    grad_value, value_sums = scatter_rows(grid, near_value, near_query, near_key, second=both)
    final["out_line"] = combine_line(grid, final["out_plane"], *both)
    output = hidden_one + jnp.concatenate([combine_last(grid, step["out_line"]) for step in steps], axis=0)
    d_parts = after([query_part, key_part, value_part], *out_sums, *value_sums)
    d_normed = [
        sum(parts) for parts in zip(*[times_turned(part, w) for part, w in zip(d_parts, w_parts)])
    ]
    d_normed = jnp.concatenate(d_normed, axis=1)
    d_high = d_normed.astype(bf16)
    d_low = (d_normed - d_high.astype(f32)).astype(bf16)
    d_normed = from_order(d_high) + from_order(d_low)
    d_resid, sum_one = norm_back(d_normed, resid, scale_one, gain_one)
    input_grad = d_hidden_one + d_resid

    sums = jnp.concatenate([grad_route, jnp.stack([sum_one, sum_two, sum_query, sum_key], axis=1)], axis=1)
    sums = jnp.pad(sums, ((0, 0), (0, lanes - sums.shape[1])))
    parts = []
    for _ in range(3):
        parts.append(sums.astype(bf16))
        sums = sums - parts[-1].astype(f32)
    sums = sum(
        lax.dot_general(turn, part, (((0,), (0,)), ((), ())), preferred_element_type=f32)
        for part in parts
    )
    sums = reduce_small(grid, sums)
    grad_gains = [sums[:, experts + k] for k in range(4)]

    shape = (micro, 1, rows, width)
    return (
        output.reshape(shape),
        input_grad.reshape(shape),
        jnp.concatenate([grad_query, grad_key, grad_value], axis=1),
        grad_wout,
        sums[:, :experts],
        *grad_gains,
        *expert_grads,
    )


def solution(mesh):
    grid = Grid(mesh.shape["expert"])
    both = ("dp", "expert")
    tokens_spec = P(None, both, None, None)
    return jax.shard_map(
        lambda *args: shards(grid, *args),
        mesh=mesh,
        in_specs=(
            tokens_spec,
            tokens_spec,
            P(None, both),
            P(both, None),
            P(both, None),
            P(both, None),
            P(both),
            P(both),
            P(both),
            P(both),
            P("expert", None, None),
            P("expert", None, None),
            P("expert", None, None),
            tokens_spec,
        ),
        out_specs=(
            tokens_spec,
            tokens_spec,
            P(both, None),
            P(both, None),
            P(both, None),
            P(both),
            P(both),
            P(both),
            P(both),
            P("expert", None, "dp"),
            P("expert", None, "dp"),
            P("expert", None, "dp"),
        ),
        check_vma=False,
    )
```

```python
import jax
import jax.numpy as jnp
import numpy as np
from jax import lax
from jax.sharding import PartitionSpec as P

HD = 128
TOP = 8


epsilon = 1e-05
theta_base = 10000.0
masked_value = -1e30
bf16 = jnp.bfloat16
f32 = jnp.float32


def rms_scale(values):
    return lax.rsqrt(jnp.mean(values * values, axis=-1, keepdims=True) + epsilon)


def rope_tables(count, offset, width):
    halfway = width // 2
    inverse = theta_base ** (-(jnp.arange(halfway, dtype=f32) * 2.0) / width)
    places = offset + jnp.arange(count, dtype=f32)
    angles = places[:, None] * inverse[None, :]
    angles = jnp.concatenate([angles, angles], axis=1)
    return (jnp.cos(angles), jnp.sin(angles))


def rotate(values, cosine, sine):
    halfway = values.shape[-1] // 2
    turned = jnp.concatenate([-values[..., halfway:], values[..., :halfway]], axis=-1)
    return values * cosine[:, None, :] + turned * sine[:, None, :]


def norm_back(incoming, values, scaling, gain):
    weighted = incoming * gain
    inner = jnp.mean(weighted * values, axis=-1, keepdims=True)
    d_values = scaling * weighted - values * scaling * scaling * scaling * inner
    return (d_values, jnp.sum(incoming * values * scaling, axis=0))


def add_low(one, two):
    return (one.astype(f32) + two.astype(f32)).astype(one.dtype)


class Grid:
    def __init__(self, owners):
        self.owners = owners
        self.dims = {16: (4, 2, 2), 64: (4, 4, 4)}.get(owners, (owners, 1, 1))
        self.strides = (self.dims[1] * self.dims[2], self.dims[2], 1)

    def place(self):
        index = lax.axis_index("expert")
        return [index // s % n for s, n in zip(self.strides, self.dims)]

    def shift(self, values, axis, by):
        n, s = self.dims[axis], self.strides[axis]
        pairs = []
        for i in range(self.owners):
            c = i // s % n
            pairs.append((i, i + ((c + by) % n - c) * s))
        return lax.ppermute(values, "expert", pairs)

    def gather(self, values, axis):
        n = self.dims[axis]
        out = [values] + [None] * (n - 1)
        ahead = n // 2
        for k in range(1, ahead + 1):
            out[k] = self.shift(out[k - 1], axis, 1)
        for k in range(1, n - ahead):
            out[n - k] = self.shift(out[(n - k + 1) % n], axis, -1)
        return out

    def scatter(self, parts, axis, last=False, earlier=()):
        n = self.dims[axis]
        ahead = n // 2
        arrived = []
        if ahead:
            total = parts[ahead]
            for k in range(ahead - 1, -1, -1):
                total = self.shift(total, axis, -1)
                if k:
                    total = add_low(total, parts[k])
            arrived.append(total)
        if n - 1 - ahead:
            total = parts[ahead + 1]
            for k in range(ahead + 2, n + 1):
                total = self.shift(total, axis, 1)
                if k < n:
                    total = add_low(total, parts[k])
            arrived.append(total)
        total = after(parts[0], *earlier).astype(f32)
        for other in arrived:
            total = total + other.astype(f32)
        return total if last else total.astype(parts[0].dtype)


def after(values, *others):
    return lax.optimization_barrier((values, *others))[0] if others else values


def swap(values):
    return lax.ppermute(values, "dp", [(0, 1), (1, 0)])


def gather_weight(grid, shard, *earlier):
    half = shard.shape[0] // 2
    columns = shard.shape[1]
    pieces = []
    along = grid.gather(after(shard, *earlier), 0)
    for part, first, second in ((slice(0, half), 2, 1), (slice(half, None), 1, 2)):
        line = jnp.stack([piece[part] for piece in along])
        plane = jnp.stack(grid.gather(line, first))
        for piece in grid.gather(plane, second):
            pieces.append(piece.reshape(-1, columns))
    own = jnp.concatenate(pieces, axis=0)
    return (own, swap(own)), along[1:]


def times(values, weight):
    half = weight[0].shape[0]
    return sum(
        jnp.dot(values[:, k * half : (k + 1) * half], weight[k], preferred_element_type=f32)
        for k in range(2)
    )


def times_turned(values, weight):
    return [
        lax.dot_general(values, part, (((1,), (1,)), ((), ())), preferred_element_type=f32)
        for part in weight
    ]


def weight_order(grid, shard_rows):
    nz, ny, nx = grid.dims
    half = shard_rows // 2
    z, y, x = grid.place()
    core = lax.axis_index("dp")
    tables = []
    for dp_r in range(2):
        a = np.stack(np.meshgrid(np.arange(ny), np.arange(nx), np.arange(nz), np.arange(half), indexing="ij"), -1).reshape(-1, 4)
        b = np.stack(np.meshgrid(np.arange(nx), np.arange(ny), np.arange(nz), np.arange(half), indexing="ij"), -1).reshape(-1, 4)
        for color, (ry, rx, rz, i) in ((0, a.T), (1, (b.T[1], b.T[0], b.T[2], b.T[3]))):
            tables.append(np.stack([np.full_like(ry, dp_r), rz, ry, rx, i + color * half]))
    t = np.concatenate(tables, axis=1).astype(np.int32)
    where = ((core + 2 - t[0]) % 2) * grid.owners
    where = where + ((z + nz - t[1]) % nz) * grid.strides[0]
    where = where + ((y + ny - t[2]) % ny) * grid.strides[1] + (x + nx - t[3]) % nx
    return (where * shard_rows + t[4]).astype(jnp.int32)


def scatter_rows(grid, kept, *earlier, second=()):
    nz, ny, nx = grid.dims
    rows, columns = kept.shape
    out = []
    sums = []
    for part, first, after_it in ((kept[: rows // 2], 1, 2), (kept[rows // 2 :], 2, 1)):
        part = part.reshape(grid.dims[first], -1, columns)
        part = [part[k] for k in range(grid.dims[first])]
        part = grid.scatter(part, first, earlier=earlier)
        part = part.reshape(grid.dims[after_it], -1, columns)
        sums.append(part)
        part = grid.scatter([part[k] for k in range(grid.dims[after_it])], after_it, earlier=second)
        part = part.reshape(nz, -1, columns)
        out.append(grid.scatter([part[k] for k in range(nz)], 0, last=True))
    return jnp.concatenate(out, axis=0), sums


def partial_product(left, right):
    half = left.shape[1] // 2
    product = lambda a: lax.dot_general(a, right, (((0,), (0,)), ((), ())), preferred_element_type=f32)
    sent = product(left[:, half:]).astype(bf16)
    near = (product(left[:, :half]) + swap(sent).astype(f32)).astype(bf16)
    return sent, near


def reduce_small(grid, values):
    half = values.shape[0] // 2
    return scatter_rows(grid, values[:half] + swap(values[half:]))[0]


def pack(table, blocks):
    return lax.dot_general(
        table, blocks, (((3,), (2,)), ((0, 1), (0, 1))), preferred_element_type=f32
    ).astype(bf16)


def unpack(table, blocks):
    return lax.dot_general(
        table, blocks, (((2,), (2,)), ((0, 1), (0, 1))), preferred_element_type=f32
    ).astype(bf16)


def spread_plane(grid, along, *earlier):
    h = along[0].shape[1] // 2
    line = jnp.stack(after(along, *earlier))
    return grid.gather(line[..., :h], 2), grid.gather(line[..., h:], 1)


def spread_packed(grid, planes, tables, *earlier):
    nz, ny, nx = grid.dims
    planes, (slots_own, slots_y, slots_x) = after((planes, tables), *earlier)
    planes = [jnp.stack(plane) for plane in planes]
    left = [pack(slots_own[0], planes[0])]
    right = [pack(slots_own[:, 0], planes[1])]
    sent = [pack(slots_y[k - 1], planes[0]) for k in range(1, ny)]
    left += [grid.shift(rows, 1, k + 1) for k, rows in enumerate(sent)]
    more = [pack(slots_x[k - 1], planes[1]) for k in range(1, nx)]
    right += [grid.shift(rows, 2, k + 1) for k, rows in enumerate(more)]
    packed = jnp.concatenate([jnp.stack(left), jnp.stack(right, axis=1)], axis=-1)
    return packed, sent + more


def combine_first(grid, packed, h):
    nz, ny, nx = grid.dims
    left = [packed[0, ..., :h]]
    left += [grid.shift(packed[k, ..., :h], 1, -k) for k in range(1, ny)]
    right = [packed[:, 0, ..., h:]]
    right += [grid.shift(packed[:, k, ..., h:], 2, -k) for k in range(1, nx)]
    return left, right


def combine_plane(received, tables, *earlier):
    received, (slots_own, slots_y, slots_x) = after((received, tables), *earlier)
    left = unpack(jnp.concatenate([slots_own[0], *slots_y], axis=2), jnp.concatenate(received[0], axis=2))
    right = unpack(jnp.concatenate([slots_own[:, 0], *slots_x], axis=2), jnp.concatenate(received[1], axis=2))
    return left, right


def combine_line(grid, planes, *earlier):
    nz, ny, nx = grid.dims
    left = grid.scatter([planes[0][k] for k in range(nx)], 2, earlier=earlier)
    right = grid.scatter([planes[1][k] for k in range(ny)], 1, earlier=earlier)
    return jnp.concatenate([left, right], axis=-1)


def combine_last(grid, line):
    return grid.scatter([line[k] for k in range(grid.dims[0])], 0, last=True)


def shards(
    grid,
    tokens,
    routes,
    prefix,
    w_qkv,
    w_out,
    w_router,
    attn_gain,
    ffn_gain,
    query_gain,
    key_gain,
    w_gate,
    w_up,
    w_down,
    cotangent,
):
    micro = tokens.shape[0]
    rows = tokens.shape[2]
    width = tokens.shape[3]
    shard_rows = w_qkv.shape[0]
    experts = w_router.shape[1]
    nz, ny, nx = grid.dims
    heads = width // HD
    count = micro * rows
    capacity = max(2, rows * TOP * 9 // (experts * 8))
    scaling = HD ** (-0.5)
    cosine, sine = rope_tables(rows, 0.0, HD)
    positions = jnp.arange(rows, dtype=jnp.int32)
    numbers = jnp.arange(experts, dtype=jnp.int32)
    core = lax.axis_index("dp")
    me = lax.axis_index("expert")
    z, y, x = grid.place()

    lanes = rows
    small = jnp.concatenate(
        [w_router] + [gain[:, None] for gain in (attn_gain, ffn_gain, query_gain, key_gain)], axis=1
    )
    small = jnp.pad(small, ((0, 0), (0, lanes - small.shape[1])))
    member = jnp.any(routes[:, 0, None, :, :] == numbers[None, :, None, None], axis=-1)
    member = member.astype(bf16).reshape(micro * experts, rows)
    table = jnp.concatenate([small, member], axis=0)
    table = jnp.stack(grid.gather(table, 0))
    table = jnp.stack(grid.gather(table, 2))
    table = jnp.stack(grid.gather(table, 1))
    small = table[:, :, :, :shard_rows].reshape(-1, lanes)
    small = jnp.concatenate([small, swap(small)], axis=0)
    t = np.stack(
        np.meshgrid(*[np.arange(n) for n in (2, ny, nx, nz, shard_rows)], indexing="ij"), -1
    ).reshape(-1, 5).T.astype(np.int32)
    where = ((core + 2 - t[0]) % 2) * grid.owners + ((z + nz - t[3]) % nz) * grid.strides[0]
    where = where + ((y + ny - t[1]) % ny) * grid.strides[1] + (x + nx - t[2]) % nx
    where = where * shard_rows + t[4]
    features = jnp.arange(width, dtype=jnp.int32)
    spot = (features[:, None] == where[None, :]).astype(bf16)
    small = jnp.dot(spot, small, preferred_element_type=f32)
    wrouter = small[:, :experts].astype(bf16)
    gain_one, gain_two, gain_query, gain_key = [small[:, experts + k] for k in range(4)]
    member = table[:, :, :, shard_rows:].reshape(ny, nx, nz, micro, experts, rows)
    triangle = (positions[:, None] <= positions[None, :]).astype(bf16)
    ranks = jnp.dot(member, triangle, preferred_element_type=f32).astype(jnp.int32) - 1
    ranks = jnp.where(member > 0, ranks, -1)
    ranks = jnp.transpose(ranks, (4, 3, 0, 1, 2, 5))
    slot_numbers = jnp.arange(capacity, dtype=jnp.int32)
    expand = lambda r: (r[..., None, :] == slot_numbers[:, None]).astype(bf16)
    pick = lambda e: lax.dynamic_index_in_dim(ranks, e, 0, keepdims=False)
    near = lambda dy, dx: (z * ny + (y + dy) % ny) * nx + (x + dx) % nx
    slots_own = expand(pick(me))
    slots_y = [expand(pick(near(k, 0))[:, 0]) for k in range(1, ny)]
    slots_x = [expand(pick(near(0, k))[:, :, 0]) for k in range(1, nx)]
    tables = [
        (slots_own[m], [s[m] for s in slots_y], [s[m] for s in slots_x]) for m in range(micro)
    ]

    order = weight_order(grid, shard_rows)
    turn = (features[:, None] == order[None, :]).astype(bf16)
    to_order = lambda v: jnp.dot(v, turn, preferred_element_type=f32).astype(bf16)
    from_order = lambda v: lax.dot_general(
        v, turn, (((1,), (1,)), ((), ())), preferred_element_type=f32
    )

    w_parts = []
    earlier = [table]
    for w in [w_qkv[:, k * width : (k + 1) * width] for k in range(3)] + [w_out]:
        gathered, earlier = gather_weight(grid, w, *earlier)
        w_parts.append(gathered)
    wout = w_parts.pop()
    g_lines = []
    for m in range(micro):
        g_lines.append(grid.gather(after(cotangent[m, 0], *earlier), 0))
        earlier = g_lines[-1][1:]
    g_planes = [
        spread_plane(grid, line, (w_parts[2] if m == 0 else wout)[0]) for m, line in enumerate(g_lines)
    ]

    resid = tokens.astype(f32).reshape(count, width)
    scale_one = rms_scale(resid)
    normed = to_order((resid * scale_one * gain_one).astype(bf16))
    query, keyed, valued = [times(normed, w) for w in w_parts]
    scale_query = rms_scale(query)
    scale_key = rms_scale(keyed)
    split = lambda v: v.reshape(micro, rows, heads, HD)
    q_heads = rotate(split(query * scale_query * gain_query), cosine, sine).astype(bf16)
    k_all = rotate(split(keyed * scale_key * gain_key), cosine, sine).astype(bf16)
    v_all = split(valued).astype(bf16)
    allowed = (positions[None, None, :] <= positions[None, :, None]) | (
        positions[None, None, :] < prefix[:, 0][:, None, None]
    )
    scores = jnp.einsum("bqhd,bkhd->bhqk", q_heads, k_all, preferred_element_type=f32) * scaling
    scores = jnp.where(allowed[:, None], scores, masked_value)
    peak = jnp.max(scores, axis=-1, keepdims=True)
    expo = jnp.exp(scores - peak)
    probs = expo / jnp.sum(expo, axis=-1, keepdims=True)
    attended = jnp.einsum("bhqk,bkhd->bqhd", probs.astype(bf16), v_all, preferred_element_type=f32)
    attended = attended.reshape(count, width).astype(bf16)
    incoming_rows = [
        spread_packed(grid, g_planes[m], tables[m], attended if m else peak)[0] for m in range(micro)
    ]
    attended = to_order(attended)
    hidden_one = resid + times(attended, wout)
    scale_two = rms_scale(hidden_one)
    normed_two = (hidden_one * scale_two * gain_two).astype(bf16)
    router = jax.nn.softmax(jnp.dot(normed_two, wrouter, preferred_element_type=f32), axis=-1)

    blocks = ny * nx * nz * capacity
    h = width // 2
    grads = []
    arrived = []
    n_lines = []
    for m in range(micro):
        rows_m = normed_two[m * rows : (m + 1) * rows]
        n_lines.append(grid.gather(after(rows_m, *(n_lines[-1][1:] if m else [])), 0))
    sent = []
    for m in range(micro):
        planes = spread_plane(grid, n_lines[m], *sent)
        got, sent = spread_packed(grid, planes, tables[m])
        arrived.append(got)
    times_t = lambda a, b: lax.dot_general(a, b, (((1,), (1,)), ((), ())), preferred_element_type=f32)
    across = lambda a, b: lax.dot_general(a, b, (((0,), (0,)), ((), ())), preferred_element_type=f32)
    at = jnp.arange(max(128, 2 * experts), dtype=jnp.int32)[None, :]
    steps = []
    for m in range(micro):
        row_in, g_in = arrived[m].reshape(blocks, width), incoming_rows[m].reshape(blocks, width)
        if m:
            row_in, g_in = after((row_in, g_in), steps[-1]["out_rows"])
        share = jax.nn.softmax(jnp.dot(row_in, wrouter, preferred_element_type=f32), axis=-1)
        share = jnp.sum(jnp.where(numbers[None, :] == me, share, 0.0), axis=-1, keepdims=True)
        gate_val = jnp.dot(row_in, w_gate[0], preferred_element_type=f32)
        up_val = jnp.dot(row_in, w_up[0], preferred_element_type=f32)
        back = jnp.dot(g_in, w_down[0], preferred_element_type=f32)
        if m:
            before = steps[-1]
            before["d_plane"] = combine_plane(before["d_first"], tables[m - 1])
            before["out_first"] = combine_first(grid, after(before["out_rows"], *before["d_plane"]), h)
            share = after(share, *before["d_plane"])
        sigmoid_val = jax.nn.sigmoid(gate_val)
        activated = gate_val * sigmoid_val
        hidden = (activated * up_val).astype(bf16)
        d_share = jnp.sum(hidden.astype(f32) * back, axis=-1, keepdims=True)
        d_hidden = back * share
        d_gate = (d_hidden * up_val * sigmoid_val * (1.0 + gate_val * (1.0 - sigmoid_val))).astype(bf16)
        d_up = (d_hidden * activated).astype(bf16)
        hidden_share = (hidden.astype(f32) * share).astype(bf16)
        d_rows = (times_t(d_gate, w_gate[0]) + times_t(d_up, w_up[0])).astype(bf16)
        high = d_share.astype(bf16)
        low = (d_share - high.astype(f32)).astype(bf16)
        extra = jnp.where(at == me, high, jnp.where(at == me + experts, low, 0.0)).astype(bf16)
        d_rows = jnp.concatenate([extra, d_rows], axis=1).reshape(ny, nx, nz, capacity, -1)
        d_first = combine_first(grid, d_rows, h + extra.shape[1])
        hidden = after(hidden, d_rows)
        if m:
            before["d_line"] = combine_line(grid, before["d_plane"])
            hidden = after(hidden, before["d_line"])
        out_rows = (times_t(hidden, w_down[0]) * share).astype(bf16)
        out_rows = out_rows.reshape(ny, nx, nz, capacity, width)
        steps.append(dict(out_rows=out_rows, d_first=d_first))
        grads.append((row_in, d_gate, d_up, g_in, hidden_share))
    before, final = steps[-2], steps[-1]
    final["d_plane"] = combine_plane(final["d_first"], tables[-1])
    final["d_line"] = combine_line(grid, final["d_plane"])
    before["out_plane"] = combine_plane(before["out_first"], tables[-2], *final["d_plane"])
    out_first = combine_first(grid, after(final["out_rows"], *final["d_plane"]), h)
    expert_sums = []
    ties = [(final["out_rows"],), final["d_plane"], (final["d_line"],)]
    for (left, right), tie in zip(((3, 4), (0, 1), (0, 2)), ties):
        grads = after(grads, *tie, *expert_sums[-1:])
        expert_sums.append(sum(across(part[left], part[right]) for part in grads))
    d_rows_back = [combine_last(grid, step["d_line"]) for step in steps]
    extra_width = d_rows_back[0].shape[1] - width
    incoming = cotangent.astype(f32).reshape(count, width)
    returned = jnp.concatenate(d_rows_back, axis=0)
    d_router = returned[:, :experts] + returned[:, experts : 2 * experts]
    d_logits = (router * (d_router - jnp.sum(router * d_router, axis=-1, keepdims=True))).astype(bf16)
    d_normed_two = returned[:, extra_width:] + jnp.einsum(
        "re,de->rd", d_logits, wrouter, preferred_element_type=f32
    )
    grad_route = jnp.einsum("rd,re->de", normed_two, d_logits, preferred_element_type=f32)
    d_norm_two, sum_two = norm_back(
        d_normed_two, hidden_one, after(scale_two, expert_sums[-1]), gain_two
    )
    d_hidden_one = incoming + d_norm_two
    d_branch = d_hidden_one.astype(bf16)
    sent, near_out = partial_product(attended, d_branch)
    d_branch = after(d_branch, sent)

    d_mixed = jnp.concatenate(times_turned(d_branch, wout), axis=1)
    d_mixed = split(from_order(d_mixed.astype(bf16)).astype(bf16))
    d_probs = jnp.einsum("bqhd,bkhd->bhqk", d_mixed, v_all, preferred_element_type=f32)
    d_values = jnp.einsum("bhqk,bqhd->bkhd", probs.astype(bf16), d_mixed, preferred_element_type=f32)
    value_part = d_values.reshape(count, width).astype(bf16)
    sent, near_value = partial_product(normed, value_part)
    inner = after(jnp.sum(probs * d_probs, axis=-1, keepdims=True), near_out, sent)
    d_scores = (probs * (d_probs - inner) * scaling).astype(bf16)
    d_queries = jnp.einsum("bhqk,bkhd->bqhd", d_scores, k_all, preferred_element_type=f32)
    d_keys = jnp.einsum("bhqk,bqhd->bkhd", d_scores, q_heads, preferred_element_type=f32)
    before["out_line"] = combine_line(grid, before["out_plane"], near_value)
    back_sine = after(-sine, near_value)
    d_query_normed = rotate(d_queries, cosine, back_sine).reshape(count, width)
    d_key_normed = rotate(d_keys, cosine, back_sine).reshape(count, width)
    d_query, sum_query = norm_back(d_query_normed, query, scale_query, gain_query)
    query_part = d_query.astype(bf16)
    sent, near_query = partial_product(normed, query_part)
    d_key, sum_key = norm_back(d_key_normed, keyed, after(scale_key, sent), gain_key)
    key_part = d_key.astype(bf16)
    sent, near_key = partial_product(normed, key_part)
    half = w_gate.shape[2] // 2
    side = after(core, near_key)
    expert_grads = []
    for total in (expert_sums[1], expert_sums[2], expert_sums[0]):
        far = lax.dynamic_slice_in_dim(total, (1 - side) * half, half, axis=1)
        near_half = lax.dynamic_slice_in_dim(total, side * half, half, axis=1)
        expert_grads.append((near_half + swap(far.astype(bf16)).astype(f32))[None])
    final["out_plane"] = combine_plane(out_first, tables[-1], near_query, near_key)
    grad_query, query_sums = scatter_rows(grid, near_query, second=expert_grads)
    grad_key, key_sums = scatter_rows(grid, near_key, second=expert_grads)
    both = [*query_sums, *key_sums]
    grad_wout, out_sums = scatter_rows(grid, near_out, near_query, near_key, second=both)
    grad_value, value_sums = scatter_rows(grid, near_value, near_query, near_key, second=both)
    final["out_line"] = combine_line(grid, final["out_plane"], *both)
    output = hidden_one + jnp.concatenate([combine_last(grid, step["out_line"]) for step in steps], axis=0)
    nothing = (near_query[0, 0] + near_key[0, 0]) * 0
    d_parts = [part + nothing for part in (query_part, key_part, value_part)]
    d_normed = [
        sum(parts) for parts in zip(*[times_turned(part, w) for part, w in zip(d_parts, w_parts)])
    ]
    d_normed = jnp.concatenate(d_normed, axis=1)
    d_high = d_normed.astype(bf16)
    d_low = (d_normed - d_high.astype(f32)).astype(bf16)
    d_normed = from_order(d_high) + from_order(d_low)
    d_resid, sum_one = norm_back(d_normed, resid, scale_one, gain_one)
    input_grad = d_hidden_one + d_resid

    sums = jnp.concatenate([grad_route, jnp.stack([sum_one, sum_two, sum_query, sum_key], axis=1)], axis=1)
    sums = jnp.pad(sums, ((0, 0), (0, lanes - sums.shape[1])))
    parts = []
    for _ in range(3):
        parts.append(sums.astype(bf16))
        sums = sums - parts[-1].astype(f32)
    sums = sum(
        lax.dot_general(turn, part, (((0,), (0,)), ((), ())), preferred_element_type=f32)
        for part in parts
    )
    sums = reduce_small(grid, sums)
    grad_gains = [sums[:, experts + k] for k in range(4)]

    shape = (micro, 1, rows, width)
    return (
        output.reshape(shape),
        input_grad.reshape(shape),
        jnp.concatenate([grad_query, grad_key, grad_value], axis=1),
        grad_wout,
        sums[:, :experts],
        *grad_gains,
        *expert_grads,
    )


def solution(mesh):
    grid = Grid(mesh.shape["expert"])
    both = ("dp", "expert")
    tokens_spec = P(None, both, None, None)
    return jax.shard_map(
        lambda *args: shards(grid, *args),
        mesh=mesh,
        in_specs=(
            tokens_spec,
            tokens_spec,
            P(None, both),
            P(both, None),
            P(both, None),
            P(both, None),
            P(both),
            P(both),
            P(both),
            P(both),
            P("expert", None, None),
            P("expert", None, None),
            P("expert", None, None),
            tokens_spec,
        ),
        out_specs=(
            tokens_spec,
            tokens_spec,
            P(both, None),
            P(both, None),
            P(both, None),
            P(both),
            P(both),
            P(both),
            P(both),
            P("expert", None, "dp"),
            P("expert", None, "dp"),
            P("expert", None, "dp"),
        ),
        check_vma=False,
    )
```
